32 devices in a mesh: dp: 4 (over z), cls: 8 (over y, x, core).
Axes of the slice: x: 2, y: 2, z: 4, core: 2. Of those that a mesh axis runs over, the one named last changes fastest.
Arguments:
- embeddings: bfloat16 [2048, 512], P(('dp', 'cls')), may hold values from -6 to 6
- labels: int32 [2048], P('dp'), may hold values from 0 to 16383
- centres: bfloat16 [32768, 512], P('cls'), may hold values from -0.25 to 0.25
- momentum: float32 [32768, 512], P('cls'), may hold values from -3 to 3
- sample_home: int32 [16384, 1], P('cls'), may hold values from 0 to 7; in each aligned block of 2048 rows (0 to 2047, 2048 to 4095, ...) at most 512 rows name the same one
- sample_row: int32 [16384], P('cls'), may hold values from 0 to 4095
Outputs:
- emb_grad: float32 [2048, 512], P(('dp', 'cls'))
- momentum_new: float32 [32768, 512], P('cls')
- centres_new: bfloat16 [32768, 512], P('cls')
The draws below stay inside these ranges and needn't reach their ends.
Inputs may be any that keep to these rules, and one draw needn't show every extreme that they name: Among the 2048 sampled columns of one class tile (aligned blocks of sample_home), at most 512 name the same home shard, and in every draw some home shard supplies exactly 512 columns of some tile.
All inputs are finite; a program needn't handle non-finite values.
Results may differ from the reference program's by a relative error of at most 0.014.
Values may be sent and summed in bfloat16 or wider, within the bound.
No kernel may reach another device: no remote copies, remote signals or barrier semaphores. Data moves between devices by JAX's collectives and lax.ppermute only.
A program may use at most 128 MiB of HBM per device.

```python
import math
import jax
import jax.numpy as jnp
import numpy as np
from jax import lax

EMBEDDING_WIDTH = 512
CLS_DEV = 4096
SAMP_DEV = 2048
ROW_DEV = 64
CAP = 512
CLASSES = 32768
SAMPLED = 16384
BATCH = 2048
N_DP = 4
N_CLS = 8


def with_ends(drawn, stream_key, smallest, largest):
    longest = drawn.shape.index(max(drawn.shape))
    spots = []
    for shift in (0, 1):
        where = [jax.random.randint(jax.random.fold_in(stream_key, axis), (), 0, length) for axis, length in enumerate(drawn.shape)]
        where[longest] = (where[longest] + shift) % drawn.shape[longest]
        spots.append(tuple(where))
    return drawn.at[spots[0]].set(smallest).at[spots[1]].set(largest)


def level_of(stream_key, extent, split, least, largest):
    def one(position, parts):
        steps = jax.random.uniform(jax.random.fold_in(jax.random.fold_in(stream_key, 6), position), (parts,), jnp.float32, least / len(split), largest / len(split))
        return jnp.repeat(jnp.exp(steps), extent[position] // parts).reshape((-1,) + (1,) * (len(extent) - position - 1))

    gain = one(*split[0])
    for cut in split[1:]:
        gain = gain * one(*cut)
    return gain


def shared_out(stream_key, own, number, rows, number_of, top, most, slope):
    sequence = jax.random.permutation(stream_key, number_of)
    heavy_load, usual = portions_of(number_of, rows * top, most, slope, True), portions_of(number_of, rows * top, most, slope, False)
    places = jnp.arange(number_of)

    def named(sizes, rotation):
        used = int((sizes > 0).sum())
        fixed = max(1, used // 4)
        moved = fixed + (places - fixed + rotation * (used - fixed)) % max(1, number_of - fixed)
        return jnp.zeros((number_of,), jnp.int32).at[sequence[jnp.where(places < fixed, places, moved)]].set(jnp.asarray(sizes, jnp.int32))

    sizes = jnp.where(number % 4 == 0, named(heavy_load, number // 4), named(usual, number - number // 4 - 1))
    mixed = jax.random.permutation(jax.random.fold_in(own, 3), number_of)
    donor, sink = mixed[0:number_of // 2 * 2:2], mixed[1:number_of // 2 * 2:2]
    room = jnp.minimum(sizes[donor] - 1, most - sizes[sink]) // 2
    room = jnp.where((donor == sequence[0]) | (sink == sequence[0]) | (sizes[sink] == 0), 0, jnp.maximum(room, 0))
    moved = jax.random.randint(jax.random.fold_in(own, 4), (number_of // 2,), 0, 1 << 20) % (room + 1)
    sizes = sizes.at[donor].add(-moved).at[sink].add(moved)
    items = jnp.searchsorted(jnp.cumsum(sizes), jnp.arange(rows * top), side="right").astype(jnp.int32)
    grid = items.reshape(top, rows).T
    grid = grid[jax.random.permutation(jax.random.fold_in(own, 1), rows)]
    rotation = jax.random.randint(jax.random.fold_in(own, 2), (rows, 1), 0, top)
    return jnp.take_along_axis(grid, (jnp.arange(top)[None, :] + rotation) % top, axis=1)


def portions_of(count, total, bound, lean, full):
    weights = [(1 << 20) // math.isqrt(grade ** lean) + 1 for grade in range(1, count + 1)]
    largest = bound if full else min(bound, max(-(-total // count), total * weights[0] // sum(weights)))
    least = 1 if total - largest >= count - 1 else 0
    given, spare = [largest] + [least] * (count - 1), total - largest - least * (count - 1)
    while spare > 0:
        free = [i for i in range(1, count) if given[i] < largest] or [i for i in range(1, count) if given[i] < bound]
        mass, remaining = sum([weights[i] for i in free]), spare
        for i in free:
            addition = min(bound - given[i], max(1, remaining * weights[i] // mass), spare)
            given[i] = given[i] + addition
            spare = spare - addition
    return np.array(given)


def scatter_about(rng, extent, width, limit, pieces=(), held_as=jnp.bfloat16):
    result = width * jax.random.normal(rng, extent, jnp.float32)
    if pieces:
        result = result * level_of(rng, extent, pieces, -0.22, 0.18)
    return jnp.clip(result, -limit, limit).astype(held_as)


def setup_inputs(seed: int = 0) -> dict:
    arg_keys = jax.random.split(jax.random.key(seed), 7)
    embeddings = scatter_about(arg_keys[0], (BATCH, EMBEDDING_WIDTH), 1.0, 6.0, ((0, 32),))
    labels = with_ends(jax.random.randint(arg_keys[1], (BATCH,), 0, SAMPLED), jax.random.fold_in(arg_keys[1], 1), 0, SAMPLED - 1).astype(jnp.int32)
    centres = scatter_about(arg_keys[2], (CLASSES, EMBEDDING_WIDTH), EMBEDDING_WIDTH ** -0.5, 0.25, ((0, 8),))
    momentum = scatter_about(arg_keys[3], (CLASSES, EMBEDDING_WIDTH), 0.5, 3.0, ((0, 8),), jnp.float32)
    sample_home_keys = jax.random.split(jax.random.fold_in(arg_keys[4], 1), SAMPLED // SAMP_DEV)
    sample_home_turns = jax.random.permutation(jax.random.fold_in(arg_keys[4], 3), SAMPLED // SAMP_DEV)
    sample_home = jax.vmap(lambda own, number: shared_out(jax.random.fold_in(arg_keys[4], 2), own, number, SAMP_DEV, N_CLS, 1, CAP, 2))(sample_home_keys, sample_home_turns).reshape((SAMPLED, 1))
    sample_row = with_ends(jax.random.randint(arg_keys[5], (SAMPLED,), 0, CLS_DEV), jax.random.fold_in(arg_keys[5], 1), 0, CLS_DEV - 1).astype(jnp.int32)
    return dict(embeddings=embeddings, labels=labels, centres=centres, momentum=momentum, sample_home=sample_home, sample_row=sample_row)


eps = 1e-06
logit_scale = 64.0
margin = 0.35
momentum_rate = 0.9
learn_rate = 0.1
weight_decay = 0.0005

def reference(embeddings, labels, centres, momentum, sample_home, sample_row):
    xfloat = embeddings.astype(jnp.float32)
    row_norm = jnp.sqrt(lax.optimization_barrier(jnp.sum(xfloat * xfloat, axis=1, keepdims=True)) + eps)
    unit_centres = xfloat / row_norm
    normalized_embedding = unit_centres.astype(jnp.bfloat16)
    columns = (sample_home[:, 0] * CLS_DEV + sample_row).astype(jnp.int32)
    fetched = centres[columns]
    wfloat = fetched.astype(jnp.float32)
    col_norm = jnp.sqrt(lax.optimization_barrier(jnp.sum(wfloat * wfloat, axis=1, keepdims=True)) + eps)
    wunit = wfloat / col_norm
    what = wunit.astype(jnp.bfloat16)
    rows_per_group = ROW_DEV * N_CLS
    grouped_embeddings = normalized_embedding.reshape(N_DP, rows_per_group, EMBEDDING_WIDTH)
    grouped_labels = labels.reshape(N_DP, rows_per_group)
    column_ids = jnp.arange(SAMPLED, dtype=jnp.int32)

    def one_group(carry, inputs):
        batch_rows, batch_labels = inputs
        cosine = lax.dot_general(batch_rows, what, (((1,), (1,)), ((), ())), preferred_element_type=jnp.float32)
        target = (batch_labels[:, None] == column_ids[None, :]).astype(jnp.float32)
        logit = logit_scale * (cosine - margin * target)
        exp_logit = jnp.exp(logit)
        denominator = lax.optimization_barrier(jnp.sum(exp_logit, axis=1, keepdims=True))
        grad_logit = (logit_scale * (exp_logit / denominator - target)).astype(jnp.bfloat16)
        dunit = jnp.dot(grad_logit, what, preferred_element_type=jnp.float32)
        partial_w = lax.dot_general(grad_logit, batch_rows, (((0,), (0,)), ((), ())), preferred_element_type=jnp.float32)
        return (carry + partial_w, dunit)
    dwhat, dunits = lax.scan(one_group, jnp.zeros((SAMPLED, EMBEDDING_WIDTH), jnp.float32), (grouped_embeddings, grouped_labels))
    dunit = dunits.reshape(N_DP * rows_per_group, EMBEDDING_WIDTH)
    emb_grad = (dunit - unit_centres * lax.optimization_barrier(jnp.sum(unit_centres * dunit, axis=1, keepdims=True))) / row_norm
    dfetched = (dwhat - wunit * lax.optimization_barrier(jnp.sum(wunit * dwhat, axis=1, keepdims=True))) / col_norm
    centre_grad = jnp.zeros((CLASSES, EMBEDDING_WIDTH), jnp.float32).at[columns].add(dfetched)
    momentum_new = momentum_rate * momentum + centre_grad + weight_decay * centres.astype(jnp.float32)
    centres_new = (centres.astype(jnp.float32) - learn_rate * momentum_new).astype(jnp.bfloat16)
    return (emb_grad, momentum_new, centres_new)
```

```python
import math

import jax
import jax.numpy as jnp
from jax import lax
from jax.experimental import pallas as pl
from jax.experimental.pallas import tpu as pltpu
from jax.sharding import PartitionSpec as P

eps = 1e-06
logit_scale = 64.0
margin = 0.35
momentum_rate = 0.9
learn_rate = 0.1
weight_decay = 0.0005

LANES = 128
VMEM_LIMIT = 48 * 1024 * 1024
bf16 = jnp.bfloat16
f32 = jnp.float32


def dot(a, b, ca, cb):
    return lax.dot_general(a, b, (((ca,), (cb,)), ((), ())), preferred_element_type=f32)


def swap(x, axis_name, m):
    n = lax.axis_size(axis_name)
    return lax.ppermute(x, axis_name, [(i, i ^ m) for i in range(n)])


def params():
    return pltpu.CompilerParams(vmem_limit_bytes=VMEM_LIMIT)


def norm_kernel(c_ref, o_ref):
    c = c_ref[...].astype(f32)
    inv = 1.0 / jnp.sqrt(jnp.sum(c * c, axis=1, keepdims=True) + eps)
    o_ref[...] = (c * inv).astype(bf16)


def normalize(centres, tile):
    rows, width = centres.shape
    return pl.pallas_call(
        norm_kernel,
        grid=(rows // tile,),
        in_specs=[pl.BlockSpec((tile, width), lambda i: (i, 0))],
        out_specs=pl.BlockSpec((tile, width), lambda i: (i, 0)),
        out_shape=jax.ShapeDtypeStruct((rows, width), bf16),
        compiler_params=params(),
        cost_estimate=pl.CostEstimate(flops=4 * rows * width, bytes_accessed=4 * rows * width, transcendentals=rows),
        name="norm",
    )(centres)


def prep_kernel(home_rows, shard_ref, tiles_ref, table_ref, lab_ref, cnt_ref, cls_ref):
    s = shard_ref[0]
    tiles, here = tiles_ref.shape
    base = s * home_rows
    blocks = home_rows // LANES
    total = jnp.zeros((LANES, blocks), f32)
    for t in range(tiles):
        h = tiles_ref[t : t + 1, :] - base
        hi = lax.shift_right_arithmetic(h, 7)
        lo = lax.bitwise_and(h, LANES - 1)
        a = (lax.broadcasted_iota(jnp.int32, (blocks, here), 0) == hi).astype(f32).astype(bf16)
        b = (lax.broadcasted_iota(jnp.int32, (LANES, here), 0) == lo).astype(f32).astype(bf16)
        total = total + dot(b, a, 1, 1)
    for k in range(blocks):
        cnt_ref[k * LANES : (k + 1) * LANES, :] = jnp.broadcast_to(total[:, k : k + 1], (LANES, LANES))
    table = table_ref[...]
    n_hi = table.shape[0]
    p0 = lax.bitwise_and(table, 255).astype(f32).astype(bf16)
    p1 = lax.bitwise_and(lax.shift_right_logical(table, 8), 255).astype(f32).astype(bf16)
    p2 = lax.shift_right_logical(table, 16).astype(f32).astype(bf16)
    chunks, _, rows = lab_ref.shape
    for j in range(chunks):
        lab = lab_ref[j]
        hi = lax.shift_right_logical(lab, 7)
        lo = lax.bitwise_and(lab, LANES - 1)
        oh = (lax.broadcasted_iota(jnp.int32, (n_hi, rows), 0) == hi).astype(f32).astype(bf16)
        g = dot(p0, oh, 0, 0) + 256.0 * dot(p1, oh, 0, 0) + 65536.0 * dot(p2, oh, 0, 0)
        pick = jnp.where(lax.broadcasted_iota(jnp.int32, (LANES, rows), 0) == lo, g, 0.0)
        cls_ref[j] = jnp.sum(pick, axis=0, keepdims=True).astype(jnp.int32) - base


def prepare(shard, tiles, labels, home_rows):
    vm = pl.BlockSpec(memory_space=pltpu.VMEM)
    table = tiles.reshape(-1, LANES)
    return pl.pallas_call(
        lambda *refs: prep_kernel(home_rows, *refs),
        in_specs=[pl.BlockSpec(memory_space=pltpu.SMEM), vm, vm, vm],
        out_specs=(vm, vm),
        out_shape=(
            jax.ShapeDtypeStruct((home_rows, LANES), f32),
            jax.ShapeDtypeStruct(labels.shape, jnp.int32),
        ),
        compiler_params=params(),
        cost_estimate=pl.CostEstimate(
            flops=2 * tiles.size * 64 * LANES, bytes_accessed=8 * tiles.size + 512 * home_rows, transcendentals=0
        ),
        name="prep",
    )(shard, tiles, table, labels)


def logits_kernel(group, rows_here, x0_ref, x1_ref, what_ref, cnt_ref, lab_ref, w_ref, den_ref, xs_ref, ut0_ref, ut1_ref, u_acc, t_acc, d_acc):
    i = pl.program_id(0)
    tile = what_ref.shape[0]
    rows = xs_ref.shape[0]
    own = 2 * rows_here

    @pl.when(i == 0)
    def _():
        for z in range(group):
            for r, ref in ((0, x0_ref), (1, x1_ref)):
                at = (2 * z + r) * rows_here
                xs_ref[at : at + rows_here, :] = ref[z]
        u_acc[...] = jnp.zeros_like(u_acc)
        t_acc[...] = jnp.zeros_like(t_acc)
        d_acc[...] = jnp.zeros_like(d_acc)

    what = what_ref[...]
    cos = dot(what, xs_ref[...], 1, 1)
    e = jnp.exp2(cos * (logit_scale * math.log2(math.e)))
    ids = lax.broadcasted_iota(jnp.int32, (tile, LANES), 0) + i * tile
    cnt = cnt_ref[...]
    cnt_t = cnt + (math.exp(-logit_scale * margin) - 1.0)
    lab = lab_ref[0]
    den = d_acc[...]
    for k in range(rows // LANES):
        cols = slice(k * LANES, (k + 1) * LANES)
        hit = ids == lab[:, cols]
        w = e[:, cols] * jnp.where(hit, cnt_t, cnt)
        d_acc[:, cols] = den[:, cols] + jnp.sum(w.reshape(tile // 8, 8, LANES), axis=0)
        wb = w.astype(bf16)
        w_ref[:, cols] = wb
        if k < own // LANES:
            u_acc[cols, :] += dot(wb, what, 0, 0)
            t_acc[cols, :] += dot(hit.astype(f32).astype(bf16), what, 0, 0)

    @pl.when(i == pl.num_programs(0) - 1)
    def _():
        den_ref[...] = jnp.sum(d_acc[...], axis=0, keepdims=True)
        for r, ref in ((0, ut0_ref), (1, ut1_ref)):
            ref[:rows_here, :] = u_acc[r * rows_here : (r + 1) * rows_here, :].astype(bf16)
            ref[rows_here:, :] = t_acc[r * rows_here : (r + 1) * rows_here, :].astype(bf16)


def logits(x0, x1, what, cnt, lab, j, tile):
    group, rows_here, width = x0.shape
    classes = what.shape[0]
    rows = 2 * group * rows_here
    own = 2 * rows_here
    whole = lambda *shape: pl.BlockSpec(shape, lambda i: (0,) * len(shape))
    return pl.pallas_call(
        lambda *refs: logits_kernel(group, rows_here, *refs),
        grid=(classes // tile,),
        in_specs=[
            whole(group, rows_here, width),
            whole(group, rows_here, width),
            pl.BlockSpec((tile, width), lambda i: (i, 0)),
            pl.BlockSpec((tile, LANES), lambda i: (i, 0)),
            pl.BlockSpec((1, 1, rows), lambda i: (j, 0, 0)),
        ],
        out_specs=(
            pl.BlockSpec((tile, rows), lambda i: (i, 0)),
            whole(1, rows),
            whole(rows, width),
            whole(own, width),
            whole(own, width),
        ),
        out_shape=(
            jax.ShapeDtypeStruct((classes, rows), bf16),
            jax.ShapeDtypeStruct((1, rows), f32),
            jax.ShapeDtypeStruct((rows, width), bf16),
            jax.ShapeDtypeStruct((own, width), bf16),
            jax.ShapeDtypeStruct((own, width), bf16),
        ),
        scratch_shapes=[
            pltpu.VMEM((own, width), f32),
            pltpu.VMEM((own, width), f32),
            pltpu.VMEM((8, rows), f32),
        ],
        compiler_params=params(),
        cost_estimate=pl.CostEstimate(
            flops=2 * rows * classes * width * 3 // 2,
            bytes_accessed=2 * rows * classes + 2 * classes * width,
            transcendentals=rows * classes,
        ),
        name="logits",
    )(x0, x1, what, cnt, lab)


def update_kernel(chunks, rate_ref, lab_ref, c_ref, m_ref, *refs):
    w_refs, x_refs, (mo_ref, co_ref) = refs[:chunks], refs[chunks : 2 * chunks], refs[2 * chunks :]
    tile = c_ref.shape[0]
    i = pl.program_id(0)
    rows = x_refs[0].shape[0]
    ids = lax.broadcasted_iota(jnp.int32, (tile, rows), 0) + i * tile
    dw = jnp.zeros(c_ref.shape, f32)
    for j in range(chunks):
        g = w_refs[j][...].astype(f32) * rate_ref[j] - jnp.where(ids == lab_ref[j], logit_scale, 0.0)
        dw = dw + dot(g.astype(bf16), x_refs[j][...], 1, 0)
    c = c_ref[...].astype(f32)
    inv = 1.0 / jnp.sqrt(jnp.sum(c * c, axis=1, keepdims=True) + eps)
    unit = c * inv
    grad = (dw - unit * jnp.sum(unit * dw, axis=1, keepdims=True)) * inv
    m = momentum_rate * m_ref[...] + grad + weight_decay * c
    mo_ref[...] = m
    co_ref[...] = (c - learn_rate * m).astype(bf16)


def update(rate, lab, centres, momentum, ws, xs, tile):
    chunks = len(ws)
    classes, width = centres.shape
    rows = xs[0].shape[0]
    whole = lambda *shape: pl.BlockSpec(shape, lambda i: (0,) * len(shape))
    block = pl.BlockSpec((tile, width), lambda i: (i, 0))
    return pl.pallas_call(
        lambda *refs: update_kernel(chunks, *refs),
        grid=(classes // tile,),
        in_specs=[whole(chunks, 1, rows), whole(chunks, 1, rows), block, block]
        + [pl.BlockSpec((tile, rows), lambda i: (i, 0))] * chunks
        + [whole(rows, width)] * chunks,
        out_specs=(block, block),
        out_shape=(
            jax.ShapeDtypeStruct((classes, width), f32),
            jax.ShapeDtypeStruct((classes, width), bf16),
        ),
        compiler_params=params(),
        cost_estimate=pl.CostEstimate(
            flops=2 * rows * chunks * classes * width,
            bytes_accessed=2 * rows * chunks * classes + 12 * classes * width,
            transcendentals=0,
        ),
        name="update",
    )(rate, lab, centres, momentum, *ws, *xs)


def body(embeddings, labels, centres, momentum, sample_home, sample_row):
    shards = lax.axis_size("cls")
    group = lax.axis_size("dp")
    chips = shards // 2
    home_rows, width = centres.shape
    rows_here = embeddings.shape[0]
    here = sample_row.shape[0]
    shard = lax.axis_index("cls")
    chunk_rows = 2 * group * rows_here

    ids = (sample_home[:, 0] * home_rows + sample_row)[None, :]
    step = 1
    while step < shards:
        ids = jnp.concatenate([ids, swap(ids, "cls", step)], axis=0)
        step *= 2

    labs = jnp.stack([labels] + [swap(labels, "dp", m) for m in range(1, group)])
    labs = (lax.bitwise_xor(labs // here, shard) * here + labs % here).reshape(group, shards, rows_here)
    bit = 1
    while bit < shards:
        labs = labs.reshape(group, shards // (2 * bit), 2, bit, rows_here)
        labs = jnp.where(lax.bitwise_and(shard, bit) != 0, labs[:, :, ::-1], labs)
        bit *= 2
    labs = labs.reshape(group, chips, 2, rows_here).transpose(1, 0, 2, 3).reshape(chips, 1, chunk_rows)

    what = normalize(centres, min(1024, home_rows))
    cnt, lab = prepare(shard.astype(jnp.int32).reshape(1), ids, labs, home_rows)

    xfloat = embeddings.astype(f32)
    row_norm = jnp.sqrt(jnp.sum(xfloat * xfloat, axis=1, keepdims=True) + eps)
    unit = xfloat / row_norm
    xhat = unit.astype(bf16)
    mine = jnp.stack([xhat] + [swap(xhat, "dp", m) for m in range(1, group)])
    mine_of = [mine] + [swap(mine, "cls", 2 * q) for q in range(1, chips)]
    other_of = [swap(x, "cls", 1) for x in mine_of]

    tile = min(1024, home_rows)
    parts = [logits(mine_of[q], other_of[q], what, cnt, lab, q, tile) for q in range(chips)]
    ws = [p[0] for p in parts]
    xs = [p[2] for p in parts]

    den = jnp.concatenate([p[1] for p in parts], axis=0)
    theirs = swap(den, "cls", 1).reshape(chips, group, 2, rows_here)[:, :, ::-1]
    den = den + theirs.reshape(chips, chunk_rows)
    got = [swap(den, "cls", 2 * q) for q in range(1, chips)]
    for q in range(1, chips):
        den = den + jnp.concatenate([got[q - 1][j ^ q][None] for j in range(chips)], axis=0)
    rate = (logit_scale / den).reshape(chips, 1, chunk_rows)

    momentum_new, centres_new = update(rate, lab, centres, momentum, ws, xs, min(512, home_rows))

    away = swap(jnp.stack([p[4] for p in parts]), "cls", 1)
    pair = [(p[3].astype(f32) + away[q].astype(f32)) for q, p in enumerate(parts)]
    total = pair[0]
    for q in range(1, chips):
        total = total + swap(pair[q].astype(bf16), "cls", 2 * q).astype(f32)
    scale = rate[0, 0, :rows_here][:, None]
    dunit = total[:rows_here] * scale - logit_scale * total[rows_here:]
    emb_grad = (dunit - unit * jnp.sum(unit * dunit, axis=1, keepdims=True)) / row_norm
    return (emb_grad, momentum_new, centres_new)


def solution(mesh):
    placed = (
        P(("dp", "cls"), None),
        P("dp"),
        P("cls", None),
        P("cls", None),
        P("cls", None),
        P("cls"),
    )
    return jax.shard_map(
        body,
        mesh=mesh,
        in_specs=placed,
        out_specs=(P(("dp", "cls"), None), P("cls", None), P("cls", None)),
        check_vma=False,
    )
```

```python
import math

import jax
import jax.numpy as jnp
from jax import lax
from jax.experimental import pallas as pl
from jax.experimental.pallas import tpu as pltpu
from jax.sharding import PartitionSpec as P

eps = 1e-06
logit_scale = 64.0
margin = 0.35
momentum_rate = 0.9
learn_rate = 0.1
weight_decay = 0.0005

LANES = 128
sharpness = logit_scale * math.log2(math.e)
HBM = pl.BlockSpec(memory_space=pltpu.HBM)
bf16 = jnp.bfloat16
f32 = jnp.float32


def dot(a, b, ca, cb):
    return lax.dot_general(a, b, (((ca,), (cb,)), ((), ())), preferred_element_type=f32)


def swap(x, axis_name, m):
    n = lax.axis_size(axis_name)
    return lax.ppermute(x, axis_name, [(i, i ^ m) for i in range(n)])


def shift(x, axis_name, m):
    n = lax.axis_size(axis_name)
    return lax.ppermute(x, axis_name, [(i, (i + m) % n) for i in range(n)])


def params(mib):
    return pltpu.CompilerParams(vmem_limit_bytes=mib << 20)


def iota(shape, axis):
    return lax.broadcasted_iota(jnp.int32, shape, axis)


def ones_where(mask):
    return mask.astype(f32).astype(bf16)


def look_up(table, hi, lo, limit):
    n_hi, n = table.shape[0], hi.shape[1]
    oh = ones_where(iota((n_hi, n), 0) == hi)
    got = jnp.zeros((LANES, n), f32)
    for bits in range(0, 8 * pieces_of(limit), 8):
        piece = lax.bitwise_and(lax.shift_right_logical(table, bits), 255).astype(f32).astype(bf16)
        got = got + float(1 << bits) * dot(piece, oh, 0, 0)
    pick = jnp.where(iota((LANES, n), 0) == lo, got, 0.0)
    return jnp.sum(pick, axis=0, keepdims=True).astype(jnp.int32)


def pieces_of(limit):
    return -(-(limit - 1).bit_length() // 8)


def tell_kernel(dims, x_ref, home_ref, row_ref, lab_ref, o_ref):
    home_rows, rows_here, _, classes, sampled = dims
    width = x_ref.shape[1]
    x = x_ref[...].astype(f32)
    scale = sharpness / jnp.sqrt(jnp.sum(x * x, axis=1, keepdims=True) + eps)
    o_ref[:rows_here, :] = (x * scale).astype(bf16)
    per = width // LANES
    lines = []
    for values, limit in ((home_ref[...] * home_rows + row_ref[...], classes), (lab_ref[...], sampled)):
        for k in range(pieces_of(limit)):
            v = lax.bitwise_and(lax.shift_right_logical(values, 8 * k), 255).astype(f32)
            for r in range(v.shape[0] // per):
                lines.append(jnp.concatenate([v[r * per + c : r * per + c + 1, :] for c in range(per)], axis=1))
    lines += [jnp.zeros_like(lines[0])] * (o_ref.shape[0] - rows_here - len(lines))
    o_ref[rows_here:, :] = jnp.concatenate(lines, axis=0).astype(bf16)


def tell(embeddings, home, row, labels, dims):
    _, rows_here, _, classes, sampled = dims
    width = embeddings.shape[1]
    lines = (row.size * pieces_of(classes) + labels.size * pieces_of(sampled)) // width
    args = [embeddings, home.reshape(-1, LANES), row.reshape(-1, LANES), labels.reshape(-1, LANES)]
    args = [pltpu.with_memory_space_constraint(x, pltpu.HBM) for x in args]
    return pl.pallas_call(
        lambda *refs: tell_kernel(dims, *refs),
        out_shape=jax.ShapeDtypeStruct((-(-(rows_here + lines) // 16) * 16, width), bf16),
        compiler_params=params(4),
        name="tell",
    )(*args)


def decode(get, row, count, number):
    total = get(row, row + count).astype(f32)
    for k in range(1, number):
        total = total + float(1 << (8 * k)) * get(row + k * count, row + (k + 1) * count).astype(f32)
    return total


def swap_groups(x, size):
    n = x.shape[1] // size
    return jnp.concatenate([x[:, (g ^ 1) * size : ((g ^ 1) + 1) * size] for g in range(n)], axis=1)


def prep_kernel(dims, shard_ref, mine_ref, away_ref, row_ref, rep_ref, cnt_ref, off_ref, known_ref, table_ref):
    home_rows, rows_here, here, classes, _ = dims
    base = shard_ref[0] * home_rows
    chips, _, width = mine_ref.shape
    blocks = home_rows // LANES
    lines, id_bytes = here // width, pieces_of(classes)
    total = jnp.zeros((LANES, blocks), f32)
    total_t = jnp.zeros((blocks, LANES), f32)
    for tile in range(2 * chips):
        ref = (mine_ref, away_ref)[tile % 2]
        ids = decode(lambda p, q: ref[tile // 2, p:q, :], rows_here, lines, id_bytes).astype(jnp.int32)
        h = ids - base
        for k in range(lines):
            a = ones_where(iota((blocks, width), 0) == lax.shift_right_arithmetic(h[k : k + 1], 7))
            b = ones_where(iota((LANES, width), 0) == lax.bitwise_and(h[k : k + 1], LANES - 1))
            total = total + dot(b, a, 1, 1)
            total_t = total_t + dot(a, b, 1, 1)
            for c in range(width // LANES):
                to = (tile * lines + k) * (width // LANES) + c
                table_ref[to : to + 1, :] = ids[k : k + 1, c * LANES : (c + 1) * LANES]
    have, have_t = ones_where(total > 0), ones_where(total_t > 0)
    before = ones_where(iota((LANES, LANES), 1) < iota((LANES, LANES), 0))
    ahead = ones_where(iota((LANES, LANES), 0) < iota((LANES, LANES), 1))
    ahead_b = ones_where(iota((blocks, blocks), 0) < iota((blocks, blocks), 1))
    before_b = ones_where(iota((blocks, blocks), 1) < iota((blocks, blocks), 0))
    sizes = jnp.broadcast_to(jnp.sum(have.astype(f32), axis=0, keepdims=True), (8, blocks))
    start = dot(sizes.astype(bf16), ahead_b, 1, 0)
    off_ref[...] = jnp.concatenate([start, start + sizes], axis=1).astype(jnp.int32)
    sizes_t = jnp.broadcast_to(jnp.sum(have_t.astype(f32), axis=1, keepdims=True), (blocks, LANES))
    start_t = dot(before_b, sizes_t.astype(bf16), 1, 0)
    pos = jnp.where(total > 0, dot(before, have, 1, 0) + start[:1], -1.0).astype(jnp.int32)
    pos_t = jnp.where(total_t > 0, dot(have_t, ahead, 1, 0) + start_t, -1.0).astype(jnp.int32)
    for k in range(blocks):
        rows = slice(k * LANES, (k + 1) * LANES)
        row_ref[k] = pos_t[k : k + 1, :]
        rep_ref[rows, :] = jnp.broadcast_to(pos[:, k : k + 1], (LANES, LANES))
        cnt_ref[rows, :] = jnp.broadcast_to(total[:, k : k + 1], (LANES, LANES))
    known_ref[...] = jnp.maximum(pos_t, 0)


def labels_kernel(dims, shard_ref, known_ref, table_ref, *refs):
    home_rows, rows_here, here, classes, sampled = dims
    z_refs, at_ref = refs[:-1], refs[-1]
    chips = at_ref.shape[0]
    width = z_refs[0].shape[1]
    shard = shard_ref[0]
    base = shard * home_rows
    lines, id_bytes = here // width, pieces_of(classes)
    known = known_ref[...]
    table = table_ref[...]
    own = 2 * rows_here
    group_rows = 2 * chips * rows_here
    lab_lines, lab_bytes = group_rows // width, pieces_of(sampled)
    per_tile = here // LANES
    for z, ref in enumerate(z_refs):
        first = rows_here + lines * id_bytes
        got = decode(lambda p, q: ref[p:q, :], first, lab_lines, lab_bytes)
        lab = jnp.concatenate([got[k : k + 1] for k in range(lab_lines)], axis=1)
        bit = 1
        while bit < 2 * chips:
            lab = jnp.where(lax.bitwise_and(shard, bit) != 0, swap_groups(lab, bit * rows_here), lab)
            bit *= 2
        lab = lab.astype(jnp.int32)
        tile = lax.bitwise_xor(lax.shift_right_logical(lab, here.bit_length() - 1), shard)
        hi = tile * per_tile + lax.shift_right_logical(lax.bitwise_and(lab, here - 1), 7)
        h = look_up(table, hi, lax.bitwise_and(lab, LANES - 1), classes) - base
        at = look_up(known, lax.shift_right_arithmetic(h, 7), lax.bitwise_and(h, LANES - 1), home_rows)
        at = jnp.where((h >= 0) & (h < home_rows), at, -1)
        for j in range(chips):
            at_ref[j, :, z * own : (z + 1) * own] = at[:, j * own : (j + 1) * own]


def prepare(shard, mine, away, dims):
    home_rows, _, _, _, sampled = dims
    vm = pl.BlockSpec(memory_space=pltpu.VMEM)
    blocks = home_rows // LANES
    i32 = jnp.int32
    return pl.pallas_call(
        lambda *refs: prep_kernel(dims, *refs),
        in_specs=[pl.BlockSpec(memory_space=pltpu.SMEM), vm, vm],
        out_specs=(vm,) * 6,
        out_shape=(
            jax.ShapeDtypeStruct((blocks, 1, LANES), i32),
            jax.ShapeDtypeStruct((home_rows, LANES), i32),
            jax.ShapeDtypeStruct((home_rows, LANES), f32),
            jax.ShapeDtypeStruct((8, 2 * blocks), i32),
            jax.ShapeDtypeStruct((blocks, LANES), i32),
            jax.ShapeDtypeStruct((sampled // LANES, LANES), i32),
        ),
        compiler_params=params(10),
        cost_estimate=pl.CostEstimate(flops=128 * sampled * LANES, bytes_accessed=1024 * home_rows, transcendentals=0),
        name="prep",
    )(shard, mine, away)


def label_places(shard, known, table, told, chips, dims):
    rows_here = dims[1]
    vm = pl.BlockSpec(memory_space=pltpu.VMEM)
    return pl.pallas_call(
        lambda *refs: labels_kernel(dims, *refs),
        in_specs=[pl.BlockSpec(memory_space=pltpu.SMEM)] + [vm] * (2 + len(told)),
        out_specs=vm,
        out_shape=jax.ShapeDtypeStruct((chips, 1, 2 * len(told) * rows_here), jnp.int32),
        compiler_params=params(12),
        cost_estimate=pl.CostEstimate(
            flops=8 * table.size * 2 * chips * len(told) * rows_here, bytes_accessed=8 * table.size, transcendentals=0
        ),
        name="places",
    )(shard, known, table, *told)


WINDOW = LANES + 16


def pack_kernel(off_ref, row_ref, cnt_ref, c_ref, what_ref, raw_ref, num_ref):
    i = pl.program_id(0)

    @pl.when(i == 0)
    def _():
        for ref in (what_ref, raw_ref, num_ref):
            ref[:16, :] = jnp.zeros((16, ref.shape[1]), ref.dtype)

    c = c_ref[...].astype(f32)
    width = c.shape[1]
    unit = (c * (1.0 / jnp.sqrt(jnp.sum(c * c, axis=1, keepdims=True) + eps))).astype(bf16)
    cnt = cnt_ref[...]
    high = jnp.floor(cnt * (1.0 / 256.0))
    low = cnt - 256.0 * high
    here = row_ref.shape[0]
    todo = []
    for k in range(here):
        rows = slice(k * LANES, (k + 1) * LANES)
        base = pl.multiple_of(lax.shift_left(lax.shift_right_logical(off_ref[0, i * here + k], 4), 4), 16)
        pick = ones_where(iota((WINDOW, LANES), 0) + base == row_ref[k])
        right = jnp.concatenate([unit[rows], c_ref[rows, :], low[rows].astype(bf16), high[rows].astype(bf16)], axis=1)
        todo.append((base, dot(pick, right, 1, 0)))
    for base, got in todo:
        num = got[:, 2 * width : 2 * width + LANES] + 256.0 * got[:, 2 * width + LANES :]
        for ref, new in ((what_ref, got[:, :width]), (raw_ref, got[:, width : 2 * width]), (num_ref, num)):
            new = new.astype(ref.dtype)
            ref[pl.ds(base, 16), :] = ref[pl.ds(base, 16), :] + new[:16]
            ref[pl.ds(pl.multiple_of(base + 16, 16), LANES), :] = new[16:]

    @pl.when(i == pl.num_programs(0) - 1)
    def _():
        for ref in (what_ref, raw_ref, num_ref):
            ref[pl.ds(pl.multiple_of(base + WINDOW, 16), 4 * LANES), :] = jnp.zeros((4 * LANES, ref.shape[1]), ref.dtype)


def pack(off, row, cnt, centres, tile):
    classes, width = centres.shape
    per = tile // LANES
    room = classes + 6 * LANES
    whole = lambda n: pl.BlockSpec((room, n), lambda i: (0, 0))
    return pl.pallas_call(
        pack_kernel,
        grid=(classes // tile,),
        in_specs=[
            pl.BlockSpec(memory_space=pltpu.SMEM),
            pl.BlockSpec((per, 1, LANES), lambda i: (i, 0, 0)),
            pl.BlockSpec((tile, LANES), lambda i: (i, 0)),
            pl.BlockSpec((tile, width), lambda i: (i, 0)),
        ],
        out_specs=(whole(width), whole(width), whole(LANES)),
        out_shape=(
            jax.ShapeDtypeStruct((room, width), bf16),
            jax.ShapeDtypeStruct((room, width), bf16),
            jax.ShapeDtypeStruct((room, LANES), f32),
        ),
        compiler_params=params(20),
        cost_estimate=pl.CostEstimate(flops=5 * classes * LANES * width, bytes_accessed=4 * classes * width, transcendentals=0),
        name="pack",
    )(off, row, cnt, centres)


def used_tile(i, steps):
    return (lax.min(i, steps[0] - 1), 0)


def logits_kernel(chunks, tile, off_ref, e0_ref, e1_ref, what_ref, num_ref, at_ref, *refs):
    l0_refs, l1_refs = refs[:chunks], refs[chunks : 2 * chunks]
    w_hbm, den_ref, turn_ref, x_ref, d_acc, cos0, cos1, w_buf, w_sem = refs[2 * chunks :]
    group, rows_here, _ = l0_refs[0].shape
    rows = cos0.shape[1]
    for j in range(chunks):
        for r, (early, late) in enumerate(((e0_ref, l0_refs[j]), (e1_ref, l1_refs[j]))):
            to = j * rows + r * rows_here
            x_ref[to : to + rows_here, :] = early[j, :rows_here, :]
            for z in range(group):
                to = j * rows + (2 * z + 2 + r) * rows_here
                x_ref[to : to + rows_here, :] = late[z]
    d_acc[...] = jnp.zeros_like(d_acc)
    used = off_ref[0, off_ref.shape[1] - 1]
    steps = lax.shift_right_logical(used + tile - 1, tile.bit_length() - 1)
    half = tile // 2

    def put(t):
        slot = lax.bitwise_and(t, 1)
        here = pl.ds(pl.multiple_of(t * tile, tile), tile)
        return pltpu.make_async_copy(w_buf.at[slot], w_hbm.at[here], w_sem.at[slot])

    def product(first, j):
        a = what_ref[pl.ds(pl.multiple_of(first, half), half), :]
        return dot(a, x_ref[pl.ds(pl.multiple_of(j * rows, rows), rows), :], 1, 1)

    def weigh(cos_ref, first, j, slot, to):
        ids = iota((half, LANES), 0) + first
        num = num_ref[pl.ds(pl.multiple_of(first, half), half), :]
        num_t = num + (math.exp(-logit_scale * margin) - 1.0)
        at = at_ref[j]
        for k in range(rows // LANES):
            cols = slice(k * LANES, (k + 1) * LANES)
            w = jnp.exp2(cos_ref[:, cols]) * jnp.where(ids == at[:, cols], num_t, num)
            d_acc[j, :, cols] += jnp.sum(w.reshape(half // 8, 8, LANES), axis=0)
            w_buf[slot, to : to + half, pl.ds(pl.multiple_of(j * rows + k * LANES, LANES), LANES)] = w.astype(bf16)

    cos0[...] = product(0, 0)

    def one(t, carry):
        @pl.when(t >= 2)
        def _():
            put(t - 2).wait()

        slot = lax.bitwise_and(t, 1)

        def chunk(j, carry):
            cos1[...] = product(t * tile + half, j)
            weigh(cos0, t * tile, j, slot, 0)
            last = j == chunks - 1
            cos0[...] = product(jnp.where(last, t + 1, t) * tile, jnp.where(last, 0, j + 1))
            weigh(cos1, t * tile + half, j, slot, half)
            return carry

        lax.fori_loop(0, chunks, chunk, 0)
        put(t).start()
        return carry

    lax.fori_loop(0, steps, one, 0)
    for back in (2, 1):

        @pl.when(steps >= back)
        def _():
            put(steps - back).wait()

    for j in range(chunks):
        den = jnp.sum(d_acc[j], axis=0, keepdims=True)
        den_ref[j] = den
        turn_ref[j] = swap_groups(den, rows_here)


def logits(off, early0, early1, late0, late1, what, num, at, tile, classes):
    chunks = len(late0)
    group, rows_here, width = late0[0].shape
    rows = 2 * (group + 1) * rows_here
    vm = pl.BlockSpec(memory_space=pltpu.VMEM)
    return pl.pallas_call(
        lambda *refs: logits_kernel(chunks, tile, *refs),
        in_specs=[pl.BlockSpec(memory_space=pltpu.SMEM)] + [vm] * (5 + 2 * chunks),
        out_specs=(HBM, vm, vm, vm),
        out_shape=(
            pltpu.HBM((classes, chunks * rows), bf16),
            jax.ShapeDtypeStruct((chunks, 1, rows), f32),
            jax.ShapeDtypeStruct((chunks, 1, rows), f32),
            jax.ShapeDtypeStruct((chunks * rows, width), bf16),
        ),
        scratch_shapes=[
            pltpu.VMEM((chunks, 8, rows), f32),
            pltpu.VMEM((tile // 2, rows), f32),
            pltpu.VMEM((tile // 2, rows), f32),
            pltpu.VMEM((2, tile, chunks * rows), bf16),
            pltpu.SemaphoreType.DMA((2,)),
        ],
        compiler_params=params(8 + 3 * chunks // 2),
        cost_estimate=pl.CostEstimate(
            flops=chunks * rows * classes * width,
            bytes_accessed=chunks * rows * classes + classes * width,
            transcendentals=chunks * rows * classes // 2,
        ),
        name="logits",
    )(off, early0, early1, what, num, at, *late0, *late1)


def own_columns(tile, own, at):
    return pl.BlockSpec((tile, own), lambda i, steps: (lax.min(i, steps[0] - 1), at))


def rows_kernel(chunks, steps_ref, what_ref, at_ref, *refs):
    w_refs, (self_ref, away_ref), acc = refs[:chunks], refs[chunks : chunks + 2], refs[chunks + 2]
    i = pl.program_id(0)
    tile = what_ref.shape[0]
    own = w_refs[0].shape[1]
    half = own // 2

    @pl.when(i == 0)
    def _():
        acc[...] = jnp.zeros_like(acc)

    @pl.when(i < steps_ref[0])
    def _():
        ids = iota((tile, own), 0) + i * tile
        left = [w[...] for w in w_refs] + [ones_where(ids == at_ref[j][:, :own]) for j in range(chunks)]
        acc[...] += dot(jnp.concatenate(left, axis=1), what_ref[...], 0, 0)

    @pl.when(i == pl.num_programs(0) - 1)
    def _():
        for j in range(chunks):
            for part in range(2):
                at = (part * chunks + j) * own
                self_ref[j, part * half : (part + 1) * half, :] = acc[at : at + half, :].astype(bf16)
                away_ref[j, part * half : (part + 1) * half, :] = acc[at + half : at + own, :].astype(bf16)


def row_parts(steps, what, at, w, own, tile):
    chunks, _, rows = at.shape
    width = what.shape[1]
    out = jax.ShapeDtypeStruct((chunks, own, width), bf16)
    whole = pl.BlockSpec((chunks, own, width), lambda i, n: (0, 0, 0))
    return pl.pallas_call(
        lambda *refs: rows_kernel(chunks, *refs),
        grid_spec=pltpu.PrefetchScalarGridSpec(
            num_scalar_prefetch=1,
            grid=(w.shape[0] // tile,),
            in_specs=[
                pl.BlockSpec((tile, width), used_tile),
                pl.BlockSpec(at.shape, lambda i, n: (0, 0, 0)),
            ]
            + [own_columns(tile, own, j * rows // own) for j in range(chunks)],
            out_specs=(whole, whole),
            scratch_shapes=[pltpu.VMEM((2 * chunks * own, width), f32)],
        ),
        out_shape=(out, out),
        compiler_params=params(8 + 3 * chunks),
        cost_estimate=pl.CostEstimate(
            flops=2 * chunks * own * w.shape[0] * width, bytes_accessed=2 * what.size, transcendentals=0
        ),
        name="rows",
    )(steps, what, at, *[w] * chunks)


def update_kernel(chunks, step, tile, off_ref, at_ref, rep_ref, raw_ref, c_hbm, m_hbm, *refs):
    w_hbm, x_ref, d_refs = refs[0], refs[1], refs[2 : 2 + chunks]
    mo_hbm, co_hbm, scale_ref, rate_ref, dw_ref, c_buf, m_buf, c_new, m_new, buf, w_sem, c_sem, m_sem, co_sem, mo_sem = refs[2 + chunks :]
    classes, width = c_buf.shape
    per = tile // LANES
    groups = classes // tile
    blocks = off_ref.shape[1] // 2
    rows = x_ref.shape[0] // chunks
    used = off_ref[0, 2 * blocks - 1]

    def span(g):
        return pl.ds(pl.multiple_of(g * tile, tile), tile)

    def ins(g):
        at = span(g)
        return (
            pltpu.make_async_copy(c_hbm.at[at], c_buf.at[at], c_sem.at[g]),
            pltpu.make_async_copy(m_hbm.at[at], m_buf.at[at], m_sem.at[g]),
        )

    def outs(g):
        at, slot = span(g), lax.bitwise_and(g, 1)
        return (
            pltpu.make_async_copy(c_new.at[slot], co_hbm.at[at], co_sem.at[slot]),
            pltpu.make_async_copy(m_new.at[slot], mo_hbm.at[at], mo_sem.at[slot]),
        )

    def fetch(start):
        slot = lax.bitwise_and(lax.shift_right_logical(start, step.bit_length() - 1), 1)
        at = pl.ds(pl.multiple_of(start, step), step)
        return slot, pltpu.make_async_copy(w_hbm.at[at], buf.at[slot], w_sem.at[slot])

    @pl.when(used > 0)
    def _():
        fetch(0)[1].start()

    for g in range(groups):
        for copy in ins(g):
            copy.start()
    for j in range(chunks):
        den = d_refs[0][j]
        for q in range(1, chunks):
            den = den + d_refs[q][j ^ q]
        rate = logit_scale / den
        rate_ref[j] = rate.astype(bf16)
        if j == 0:
            scale_ref[...] = rate

    def one(done):
        @pl.when(done + step < used)
        def _():
            fetch(done + step)[1].start()

        slot, copy = fetch(done)
        at = pl.ds(pl.multiple_of(done, step), step)
        copy.wait()
        exact = min(step, 256)
        ids = iota((exact, rows), 0).astype(f32).astype(bf16)
        lines = []
        for h in range(0, step, exact):
            parts = []
            for j in range(chunks):
                place = at_ref[j] - (done + h)
                place = jnp.where((place >= 0) & (place < exact), place, -1).astype(f32).astype(bf16)
                g = buf[slot, h : h + exact, j * rows : (j + 1) * rows] * rate_ref[j]
                parts.append(jnp.where(ids == place, g - jnp.asarray(logit_scale, bf16), g))
            lines.append(jnp.concatenate(parts, axis=1))
        dw = dot(jnp.concatenate(lines, axis=0), x_ref[...], 1, 0)
        c = raw_ref[at, :].astype(f32)
        inv = 1.0 / jnp.sqrt(jnp.sum(c * c, axis=1, keepdims=True) + eps)
        along = jnp.sum(c * dw, axis=1, keepdims=True) * (inv * inv)
        dw_ref[at, :] = ((dw - c * along) * (inv * (1.0 / sharpness))).astype(bf16)
        dw_ref[pl.ds(pl.multiple_of(done + step, step), 2 * LANES), :] = jnp.zeros((2 * LANES, width), bf16)
        return done + step

    def group(g, done):
        done = lax.while_loop(lambda d: d < off_ref[0, blocks + (g + 1) * per - 1], one, done)
        for copy in ins(g):
            copy.wait()
        slot = lax.bitwise_and(g, 1)

        @pl.when(g >= 2)
        def _():
            for copy in outs(g - 2):
                copy.wait()

        lane = iota((LANES, LANES), 1)
        for k in range(per):
            base = pl.multiple_of(lax.shift_left(lax.shift_right_logical(off_ref[0, g * per + k], 4), 4), 16)
            mine = pl.ds(pl.multiple_of(g * tile + k * LANES, LANES), LANES)
            to = slice(k * LANES, (k + 1) * LANES)
            place = rep_ref[mine, :] - base
            place = jnp.concatenate([ones_where(place == lane), ones_where(place == lane + LANES)], axis=1)
            dw = dot(place, dw_ref[pl.ds(base, 2 * LANES), :], 1, 0)
            c = c_buf[mine, :].astype(f32)
            m = momentum_rate * m_buf[mine, :] + dw + weight_decay * c
            m_new[slot, to, :] = m
            c_new[slot, to, :] = (c - learn_rate * m).astype(bf16)
        for copy in outs(g):
            copy.start()
        return done

    @pl.when(used == 0)
    def _():
        dw_ref[: 2 * LANES, :] = jnp.zeros((2 * LANES, width), bf16)

    lax.fori_loop(0, groups, group, 0)
    for g in range(max(0, groups - 2), groups):
        for copy in outs(g):
            copy.wait()


def update(off, at, rep, raw, centres, momentum, w, x, dens, tile, step):
    chunks = len(dens)
    classes, width = centres.shape
    rows = x.shape[0] // chunks
    vm = pl.BlockSpec(memory_space=pltpu.VMEM)
    sems = pltpu.SemaphoreType.DMA((classes // tile,))
    return pl.pallas_call(
        lambda *refs: update_kernel(chunks, step, tile, *refs),
        in_specs=[pl.BlockSpec(memory_space=pltpu.SMEM), vm, vm, vm, HBM, HBM, HBM] + [vm] * (1 + chunks),
        out_specs=(HBM, HBM, vm),
        out_shape=(
            jax.ShapeDtypeStruct((classes, width), f32),
            jax.ShapeDtypeStruct((classes, width), bf16),
            jax.ShapeDtypeStruct((1, rows), f32),
        ),
        scratch_shapes=[
            pltpu.VMEM((chunks, 1, rows), bf16),
            pltpu.VMEM((classes + 2 * LANES + step, width), bf16),
            pltpu.VMEM((classes, width), bf16),
            pltpu.VMEM((classes, width), f32),
            pltpu.VMEM((2, tile, width), bf16),
            pltpu.VMEM((2, tile, width), f32),
            pltpu.VMEM((2, step, chunks * rows), bf16),
            pltpu.SemaphoreType.DMA((2,)),
            sems,
            sems,
            pltpu.SemaphoreType.DMA((2,)),
            pltpu.SemaphoreType.DMA((2,)),
        ],
        compiler_params=params(22 + 3 * chunks),
        cost_estimate=pl.CostEstimate(
            flops=rows * chunks * classes * width,
            bytes_accessed=rows * chunks * classes + 12 * classes * width,
            transcendentals=0,
        ),
        name="update",
    )(off, at, rep, raw, centres, momentum, w, x, *dens)


def body(embeddings, labels, centres, momentum, sample_home, sample_row):
    shards = lax.axis_size("cls")
    group = lax.axis_size("dp")
    chips = shards // 2
    home_rows, _ = centres.shape
    rows_here = embeddings.shape[0]
    here = sample_row.shape[0]
    classes, sampled = shards * home_rows, shards * here
    shard = lax.axis_index("cls")

    dims = (home_rows, rows_here, here, classes, sampled)
    told = tell(embeddings, sample_home, sample_row, labels, dims)

    from_z = [shift(told, "dp", m) for m in (1, group - 1)] + [shift(told, "dp", m) for m in range(2, group - 1)]
    early = jnp.stack([told] + [swap(told, "cls", 2 * q) for q in range(1, chips)])
    early_away = swap(early, "cls", 1)
    late0 = jnp.stack([z[:rows_here] for z in from_z])
    late = [late0] + [swap(late0, "cls", 2 * q) for q in range(1, chips)]
    late_away = []
    for x in late:
        late_away.append(swap(x, "cls", 1))

    me = shard.astype(jnp.int32).reshape(1)
    in_hbm = lambda x: pltpu.with_memory_space_constraint(x, pltpu.HBM)
    row, rep, cnt, off, known, table = prepare(me, early, early_away, dims)
    what, raw, num = pack(off, row, cnt, in_hbm(centres), min(1024, home_rows))
    at = label_places(me, known, table, [told] + from_z, chips, dims)
    tile = min(512, home_rows)
    w, own_den, turned, x = logits(off, early, early_away, late, late_away, what, num, at, tile, home_rows)
    w = in_hbm(w)

    den = own_den + swap(turned, "cls", 1)
    dens = [den] + [swap(den, "cls", 2 * q) for q in range(1, chips)]

    steps = lax.max(lax.shift_right_logical(off[0, -1:] + tile - 1, tile.bit_length() - 1), 1)
    self_part, away_part = row_parts(steps, what, at, w, 2 * rows_here, tile)
    pair = self_part.astype(f32) + swap(away_part, "cls", 1).astype(f32)
    sums = [swap(pair[q].astype(bf16), "cls", 2 * q) for q in range(1, chips)]

    momentum_new, centres_new, scale = update(
        off, at, rep, raw, in_hbm(centres), in_hbm(momentum), w, x, dens, min(512, home_rows), 512
    )
    total = pair[0]
    for got in sums:
        total = total + got.astype(f32)
    xfloat = embeddings.astype(f32)
    row_norm = jnp.sqrt(jnp.sum(xfloat * xfloat, axis=1, keepdims=True) + eps)
    unit = xfloat / row_norm
    scale = scale[0, :rows_here][:, None]
    dunit = total[:rows_here] * scale - logit_scale * total[rows_here:]
    emb_grad = (dunit - unit * jnp.sum(unit * dunit, axis=1, keepdims=True)) / row_norm
    return (emb_grad, momentum_new, centres_new)


def solution(mesh):
    placed = (
        P(("dp", "cls"), None),
        P("dp"),
        P("cls", None),
        P("cls", None),
        P("cls", None),
        P("cls"),
    )
    return jax.shard_map(
        body,
        mesh=mesh,
        in_specs=placed,
        out_specs=(P(("dp", "cls"), None), P("cls", None), P("cls", None)),
        check_vma=False,
    )
```

```python
import math

import jax
import jax.numpy as jnp
from jax import lax
from jax.experimental import pallas as pl
from jax.experimental.pallas import tpu as pltpu
from jax.sharding import PartitionSpec as P

eps = 1e-06
logit_scale = 64.0
margin = 0.35
momentum_rate = 0.9
learn_rate = 0.1
weight_decay = 0.0005

LANES = 128
sharpness = logit_scale * math.log2(math.e)
HBM = pl.BlockSpec(memory_space=pltpu.HBM)
bf16 = jnp.bfloat16
f32 = jnp.float32


def dot(a, b, ca, cb):
    return lax.dot_general(a, b, (((ca,), (cb,)), ((), ())), preferred_element_type=f32)


def swap(x, axis_name, m):
    n = lax.axis_size(axis_name)
    return lax.ppermute(x, axis_name, [(i, i ^ m) for i in range(n)])


def shift(x, axis_name, m):
    n = lax.axis_size(axis_name)
    return lax.ppermute(x, axis_name, [(i, (i + m) % n) for i in range(n)])


def params(mib):
    return pltpu.CompilerParams(vmem_limit_bytes=mib << 20)


def iota(shape, axis):
    return lax.broadcasted_iota(jnp.int32, shape, axis)


def ones_where(mask):
    return mask.astype(f32).astype(bf16)


def look_up(table, hi, lo, limit):
    n_hi, n = table.shape[0], hi.shape[1]
    oh = ones_where(iota((n_hi, n), 0) == hi)
    got = jnp.zeros((LANES, n), f32)
    for bits in range(0, 8 * pieces_of(limit), 8):
        piece = lax.bitwise_and(lax.shift_right_logical(table, bits), 255).astype(f32).astype(bf16)
        got = got + float(1 << bits) * dot(piece, oh, 0, 0)
    pick = jnp.where(iota((LANES, n), 0) == lo, got, 0.0)
    return jnp.sum(pick, axis=0, keepdims=True).astype(jnp.int32)


def pieces_of(limit):
    return -(-(limit - 1).bit_length() // 8)


def tell_kernel(dims, x_ref, home_ref, row_ref, lab_ref, o_ref):
    home_rows, rows_here, _, classes, sampled = dims
    width = x_ref.shape[1]
    x = x_ref[...].astype(f32)
    scale = sharpness / jnp.sqrt(jnp.sum(x * x, axis=1, keepdims=True) + eps)
    o_ref[:rows_here, :] = (x * scale).astype(bf16)
    per = width // LANES
    lines = []
    for values, limit in ((home_ref[...] * home_rows + row_ref[...], classes), (lab_ref[...], sampled)):
        for k in range(pieces_of(limit)):
            v = lax.bitwise_and(lax.shift_right_logical(values, 8 * k), 255).astype(f32)
            for r in range(v.shape[0] // per):
                lines.append(jnp.concatenate([v[r * per + c : r * per + c + 1, :] for c in range(per)], axis=1))
    lines += [jnp.zeros_like(lines[0])] * (o_ref.shape[0] - rows_here - len(lines))
    o_ref[rows_here:, :] = jnp.concatenate(lines, axis=0).astype(bf16)


def tell(embeddings, home, row, labels, dims):
    _, rows_here, _, classes, sampled = dims
    width = embeddings.shape[1]
    lines = (row.size * pieces_of(classes) + labels.size * pieces_of(sampled)) // width
    args = [embeddings, home.reshape(-1, LANES), row.reshape(-1, LANES), labels.reshape(-1, LANES)]
    args = [pltpu.with_memory_space_constraint(x, pltpu.HBM) for x in args]
    return pl.pallas_call(
        lambda *refs: tell_kernel(dims, *refs),
        out_shape=jax.ShapeDtypeStruct((-(-(rows_here + lines) // 16) * 16, width), bf16),
        compiler_params=params(4),
        name="tell",
    )(*args)


def decode(get, row, count, number):
    total = get(row, row + count).astype(f32)
    for k in range(1, number):
        total = total + float(1 << (8 * k)) * get(row + k * count, row + (k + 1) * count).astype(f32)
    return total


def swap_groups(x, size):
    n = x.shape[1] // size
    return jnp.concatenate([x[:, (g ^ 1) * size : ((g ^ 1) + 1) * size] for g in range(n)], axis=1)


def prep_kernel(dims, shard_ref, mine_ref, away_ref, row_ref, rep_ref, cnt_ref, off_ref, known_ref, table_ref):
    home_rows, rows_here, here, classes, _ = dims
    base = shard_ref[0] * home_rows
    chips, _, width = mine_ref.shape
    blocks = home_rows // LANES
    lines, id_bytes = here // width, pieces_of(classes)
    total = jnp.zeros((LANES, blocks), f32)
    total_t = jnp.zeros((blocks, LANES), f32)
    for tile in range(2 * chips):
        ref = (mine_ref, away_ref)[tile % 2]
        ids = decode(lambda p, q: ref[tile // 2, p:q, :], rows_here, lines, id_bytes).astype(jnp.int32)
        h = ids - base
        for k in range(lines):
            a = ones_where(iota((blocks, width), 0) == lax.shift_right_arithmetic(h[k : k + 1], 7))
            b = ones_where(iota((LANES, width), 0) == lax.bitwise_and(h[k : k + 1], LANES - 1))
            total = total + dot(b, a, 1, 1)
            total_t = total_t + dot(a, b, 1, 1)
            for c in range(width // LANES):
                to = (tile * lines + k) * (width // LANES) + c
                table_ref[to : to + 1, :] = ids[k : k + 1, c * LANES : (c + 1) * LANES]
    have, have_t = ones_where(total > 0), ones_where(total_t > 0)
    before = ones_where(iota((LANES, LANES), 1) < iota((LANES, LANES), 0))
    ahead = ones_where(iota((LANES, LANES), 0) < iota((LANES, LANES), 1))
    ahead_b = ones_where(iota((blocks, blocks), 0) < iota((blocks, blocks), 1))
    before_b = ones_where(iota((blocks, blocks), 1) < iota((blocks, blocks), 0))
    sizes = jnp.broadcast_to(jnp.sum(have.astype(f32), axis=0, keepdims=True), (8, blocks))
    start = dot(sizes.astype(bf16), ahead_b, 1, 0)
    off_ref[...] = jnp.concatenate([start, start + sizes], axis=1).astype(jnp.int32)
    sizes_t = jnp.broadcast_to(jnp.sum(have_t.astype(f32), axis=1, keepdims=True), (blocks, LANES))
    start_t = dot(before_b, sizes_t.astype(bf16), 1, 0)
    pos = jnp.where(total > 0, dot(before, have, 1, 0) + start[:1], -1.0).astype(jnp.int32)
    pos_t = jnp.where(total_t > 0, dot(have_t, ahead, 1, 0) + start_t, -1.0).astype(jnp.int32)
    for k in range(blocks):
        rows = slice(k * LANES, (k + 1) * LANES)
        row_ref[k] = pos_t[k : k + 1, :]
        rep_ref[rows, :] = jnp.broadcast_to(pos[:, k : k + 1], (LANES, LANES))
        cnt_ref[rows, :] = jnp.broadcast_to(total[:, k : k + 1], (LANES, LANES))
    known_ref[...] = jnp.maximum(pos_t, 0)


def labels_kernel(dims, shard_ref, known_ref, table_ref, *refs):
    home_rows, rows_here, here, classes, sampled = dims
    z_refs, at_ref = refs[:-1], refs[-1]
    chips = at_ref.shape[0]
    width = z_refs[0].shape[1]
    shard = shard_ref[0]
    base = shard * home_rows
    lines, id_bytes = here // width, pieces_of(classes)
    known = known_ref[...]
    table = table_ref[...]
    own = 2 * rows_here
    group_rows = 2 * chips * rows_here
    lab_lines, lab_bytes = group_rows // width, pieces_of(sampled)
    per_tile = here // LANES
    for z, ref in enumerate(z_refs):
        first = rows_here + lines * id_bytes
        got = decode(lambda p, q: ref[p:q, :], first, lab_lines, lab_bytes)
        lab = jnp.concatenate([got[k : k + 1] for k in range(lab_lines)], axis=1)
        bit = 1
        while bit < 2 * chips:
            lab = jnp.where(lax.bitwise_and(shard, bit) != 0, swap_groups(lab, bit * rows_here), lab)
            bit *= 2
        lab = lab.astype(jnp.int32)
        tile = lax.bitwise_xor(lax.shift_right_logical(lab, here.bit_length() - 1), shard)
        hi = tile * per_tile + lax.shift_right_logical(lax.bitwise_and(lab, here - 1), 7)
        h = look_up(table, hi, lax.bitwise_and(lab, LANES - 1), classes) - base
        at = look_up(known, lax.shift_right_arithmetic(h, 7), lax.bitwise_and(h, LANES - 1), home_rows)
        at = jnp.where((h >= 0) & (h < home_rows), at, -1)
        for j in range(chips):
            at_ref[j, :, z * own : (z + 1) * own] = at[:, j * own : (j + 1) * own]


def prepare(shard, mine, away, dims):
    home_rows, _, _, _, sampled = dims
    vm = pl.BlockSpec(memory_space=pltpu.VMEM)
    blocks = home_rows // LANES
    i32 = jnp.int32
    return pl.pallas_call(
        lambda *refs: prep_kernel(dims, *refs),
        in_specs=[pl.BlockSpec(memory_space=pltpu.SMEM), vm, vm],
        out_specs=(vm,) * 6,
        out_shape=(
            jax.ShapeDtypeStruct((blocks, 1, LANES), i32),
            jax.ShapeDtypeStruct((home_rows, LANES), i32),
            jax.ShapeDtypeStruct((home_rows, LANES), f32),
            jax.ShapeDtypeStruct((8, 2 * blocks), i32),
            jax.ShapeDtypeStruct((blocks, LANES), i32),
            jax.ShapeDtypeStruct((sampled // LANES, LANES), i32),
        ),
        compiler_params=params(10),
        cost_estimate=pl.CostEstimate(flops=128 * sampled * LANES, bytes_accessed=1024 * home_rows, transcendentals=0),
        name="prep",
    )(shard, mine, away)


def label_places(shard, known, table, told, chips, dims):
    rows_here = dims[1]
    vm = pl.BlockSpec(memory_space=pltpu.VMEM)
    return pl.pallas_call(
        lambda *refs: labels_kernel(dims, *refs),
        in_specs=[pl.BlockSpec(memory_space=pltpu.SMEM)] + [vm] * (2 + len(told)),
        out_specs=vm,
        out_shape=jax.ShapeDtypeStruct((chips, 1, 2 * len(told) * rows_here), jnp.int32),
        compiler_params=params(12),
        cost_estimate=pl.CostEstimate(
            flops=8 * table.size * 2 * chips * len(told) * rows_here, bytes_accessed=8 * table.size, transcendentals=0
        ),
        name="places",
    )(shard, known, table, *told)


WINDOW = LANES + 16


def pack_kernel(off_ref, row_ref, cnt_ref, c_ref, what_ref, raw_ref, num_ref):
    i = pl.program_id(0)

    @pl.when(i == 0)
    def _():
        for ref in (what_ref, raw_ref, num_ref):
            ref[:16, :] = jnp.zeros((16, ref.shape[1]), ref.dtype)

    c = c_ref[...].astype(f32)
    width = c.shape[1]
    unit = (c * (1.0 / jnp.sqrt(jnp.sum(c * c, axis=1, keepdims=True) + eps))).astype(bf16)
    cnt = cnt_ref[...]
    high = jnp.floor(cnt * (1.0 / 256.0))
    low = cnt - 256.0 * high
    here = row_ref.shape[0]
    todo = []
    for k in range(here):
        rows = slice(k * LANES, (k + 1) * LANES)
        base = pl.multiple_of(lax.shift_left(lax.shift_right_logical(off_ref[0, i * here + k], 4), 4), 16)
        pick = ones_where(iota((WINDOW, LANES), 0) + base == row_ref[k])
        right = jnp.concatenate([unit[rows], c_ref[rows, :], low[rows].astype(bf16), high[rows].astype(bf16)], axis=1)
        todo.append((base, dot(pick, right, 1, 0)))
    for base, got in todo:
        num = got[:, 2 * width : 2 * width + LANES] + 256.0 * got[:, 2 * width + LANES :]
        for ref, new in ((what_ref, got[:, :width]), (raw_ref, got[:, width : 2 * width]), (num_ref, num)):
            new = new.astype(ref.dtype)
            ref[pl.ds(base, 16), :] = ref[pl.ds(base, 16), :] + new[:16]
            ref[pl.ds(pl.multiple_of(base + 16, 16), LANES), :] = new[16:]

    @pl.when(i == pl.num_programs(0) - 1)
    def _():
        for ref in (what_ref, raw_ref, num_ref):
            ref[pl.ds(pl.multiple_of(base + WINDOW, 16), 4 * LANES), :] = jnp.zeros((4 * LANES, ref.shape[1]), ref.dtype)


def pack(off, row, cnt, centres, tile):
    classes, width = centres.shape
    per = tile // LANES
    room = classes + 6 * LANES
    whole = lambda n: pl.BlockSpec((room, n), lambda i: (0, 0))
    return pl.pallas_call(
        pack_kernel,
        grid=(classes // tile,),
        in_specs=[
            pl.BlockSpec(memory_space=pltpu.SMEM),
            pl.BlockSpec((per, 1, LANES), lambda i: (i, 0, 0)),
            pl.BlockSpec((tile, LANES), lambda i: (i, 0)),
            pl.BlockSpec((tile, width), lambda i: (i, 0)),
        ],
        out_specs=(whole(width), whole(width), whole(LANES)),
        out_shape=(
            jax.ShapeDtypeStruct((room, width), bf16),
            jax.ShapeDtypeStruct((room, width), bf16),
            jax.ShapeDtypeStruct((room, LANES), f32),
        ),
        compiler_params=params(20),
        cost_estimate=pl.CostEstimate(flops=5 * classes * LANES * width, bytes_accessed=4 * classes * width, transcendentals=0),
        name="pack",
    )(off, row, cnt, centres)


def tiles_used(off, tile):
    return lax.shift_right_logical(off[0, off.shape[1] - 1] + tile - 1, tile.bit_length() - 1)


def last_used(i, off, tile):
    return lax.max(lax.min(i, tiles_used(off, tile) - 1), 0)


def logits_kernel(chunks, tile, off_ref, e0_ref, e1_ref, what_ref, num_ref, at_ref, *refs):
    l0_refs, l1_refs = refs[:chunks], refs[chunks : 2 * chunks]
    w_hbm, den_ref, turn_ref, x_ref, d_acc, w_buf, w_sem = refs[2 * chunks :]
    group, rows_here, _ = l0_refs[0].shape
    rows = 2 * (group + 1) * rows_here
    for j in range(chunks):
        for r, (early, late) in enumerate(((e0_ref, l0_refs[j]), (e1_ref, l1_refs[j]))):
            to = j * rows + r * rows_here
            x_ref[to : to + rows_here, :] = early[j, :rows_here, :]
            for z in range(group):
                to = j * rows + (2 * z + 2 + r) * rows_here
                x_ref[to : to + rows_here, :] = late[z]
    d_acc[...] = jnp.zeros_like(d_acc)
    steps = tiles_used(off_ref, tile)
    half = tile // 2
    cut = rows

    def put(t):
        slot = lax.bitwise_and(t, 1)
        here = pl.ds(pl.multiple_of(t * tile, tile), tile)
        return pltpu.make_async_copy(w_buf.at[slot], w_hbm.at[here], w_sem.at[slot])

    def weigh(first, size, j, slot):
        here = pl.ds(pl.multiple_of(first, half), size)
        ids = iota((size, LANES), 0) + first
        num = num_ref[here, :]
        num_t = num + (math.exp(-logit_scale * margin) - 1.0)
        at = at_ref[j]
        for left in range(0, rows, cut):
            x = x_ref[pl.ds(pl.multiple_of(j * rows + left, cut), cut), :]
            cos = dot(what_ref[here, :], x, 1, 1)
            for k in range(0, cut, LANES):
                cols = slice(left + k, left + k + LANES)
                w = jnp.exp2(cos[:, k : k + LANES]) * jnp.where(ids == at[:, cols], num_t, num)
                d_acc[j, :, cols] += jnp.sum(w.reshape(size // 8, 8, LANES), axis=0)
                w_buf[slot, :size, pl.ds(pl.multiple_of(j * rows + left + k, LANES), LANES)] = w.astype(bf16)

    def one(t, size):
        @pl.when(t >= 2)
        def _():
            put(t - 2).wait()

        slot = lax.bitwise_and(t, 1)
        if size < tile:
            w_buf[slot, size:, :] = jnp.zeros((tile - size, w_buf.shape[2]), bf16)

        together = math.gcd(chunks, 4)

        def chunk(j, carry):
            for k in range(together):
                weigh(t * tile, size, j * together + k, slot)
            return carry

        lax.fori_loop(0, chunks // together, chunk, 0)
        put(t).start()

    def full(t, carry):
        one(t, tile)
        return carry

    used = off_ref[0, off_ref.shape[1] - 1]
    whole = lax.shift_right_logical(used + half - 1, tile.bit_length() - 1)
    lax.fori_loop(0, whole, full, 0)

    @pl.when(whole < steps)
    def _():
        one(whole, half)

    for back in (2, 1):

        @pl.when(steps >= back)
        def _():
            put(steps - back).wait()

    for j in range(chunks):
        den = jnp.sum(d_acc[j], axis=0, keepdims=True)
        den_ref[j] = den
        turn_ref[j] = swap_groups(den, rows_here)


def logits(off, early0, early1, late0, late1, what, num, at, tile, classes):
    chunks = len(late0)
    group, rows_here, width = late0[0].shape
    rows = 2 * (group + 1) * rows_here
    vm = pl.BlockSpec(memory_space=pltpu.VMEM)
    return pl.pallas_call(
        lambda *refs: logits_kernel(chunks, tile, *refs),
        in_specs=[pl.BlockSpec(memory_space=pltpu.SMEM)] + [vm] * (5 + 2 * chunks),
        out_specs=(HBM, vm, vm, vm),
        out_shape=(
            pltpu.HBM((classes, chunks * rows), bf16),
            jax.ShapeDtypeStruct((chunks, 1, rows), f32),
            jax.ShapeDtypeStruct((chunks, 1, rows), f32),
            jax.ShapeDtypeStruct((chunks * rows, width), bf16),
        ),
        scratch_shapes=[
            pltpu.VMEM((chunks, 8, rows), f32),
            pltpu.VMEM((2, tile, chunks * rows), bf16),
            pltpu.SemaphoreType.DMA((2,)),
        ],
        compiler_params=params(8 + 3 * chunks // 2),
        cost_estimate=pl.CostEstimate(
            flops=chunks * rows * classes * width,
            bytes_accessed=chunks * rows * classes + classes * width,
            transcendentals=chunks * rows * classes // 2,
        ),
        name="logits",
    )(off, early0, early1, what, num, at, *late0, *late1)


def own_columns(tile, own, at):
    return pl.BlockSpec((tile, own), lambda i, off: (last_used(i, off, tile), at))


def rows_kernel(chunks, off_ref, what_ref, at_ref, *refs):
    w_refs, (self_ref, away_ref), acc = refs[:chunks], refs[chunks : chunks + 2], refs[chunks + 2]
    i = pl.program_id(0)
    tile = what_ref.shape[0]
    own = w_refs[0].shape[1]
    half = own // 2

    @pl.when(i == 0)
    def _():
        acc[...] = jnp.zeros_like(acc)

    left = off_ref[0, off_ref.shape[1] - 1] - i * tile

    def add(size):
        ids = iota((size, own), 0) + i * tile
        a = [w[:size, :] for w in w_refs] + [ones_where(ids == at_ref[j][:, :own]) for j in range(chunks)]
        acc[...] += dot(jnp.concatenate(a, axis=1), what_ref[:size, :], 0, 0)

    @pl.when(left > tile // 2)
    def _():
        add(tile)

    @pl.when((left > 0) & (left <= tile // 2))
    def _():
        add(tile // 2)

    @pl.when(i == pl.num_programs(0) - 1)
    def _():
        for j in range(chunks):
            for part in range(2):
                at = (part * chunks + j) * own
                self_ref[j, part * half : (part + 1) * half, :] = acc[at : at + half, :].astype(bf16)
                away_ref[j, part * half : (part + 1) * half, :] = acc[at + half : at + own, :].astype(bf16)


def row_parts(off, what, at, w, own, tile):
    chunks, _, rows = at.shape
    width = what.shape[1]
    out = jax.ShapeDtypeStruct((chunks, own, width), bf16)
    whole = pl.BlockSpec((chunks, own, width), lambda i, n: (0, 0, 0))
    return pl.pallas_call(
        lambda *refs: rows_kernel(chunks, *refs),
        grid_spec=pltpu.PrefetchScalarGridSpec(
            num_scalar_prefetch=1,
            grid=(w.shape[0] // tile,),
            in_specs=[
                pl.BlockSpec((tile, width), lambda i, off: (last_used(i, off, tile), 0)),
                pl.BlockSpec(at.shape, lambda i, n: (0, 0, 0)),
            ]
            + [own_columns(tile, own, j * rows // own) for j in range(chunks)],
            out_specs=(whole, whole),
            scratch_shapes=[pltpu.VMEM((2 * chunks * own, width), f32)],
        ),
        out_shape=(out, out),
        compiler_params=params(8 + 3 * chunks),
        cost_estimate=pl.CostEstimate(
            flops=2 * chunks * own * w.shape[0] * width, bytes_accessed=2 * what.size, transcendentals=0
        ),
        name="rows",
    )(off, what, at, *[w] * chunks)


def update_kernel(chunks, step, tile, off_ref, at_ref, rep_ref, raw_ref, c_hbm, m_hbm, *refs):
    w_hbm, x_ref, d_refs = refs[0], refs[1], refs[2 : 2 + chunks]
    mo_hbm, co_hbm, scale_ref, rate_ref, dw_ref, c_buf, m_buf, c_new, m_new, buf, w_sem, c_sem, m_sem, co_sem, mo_sem = refs[2 + chunks :]
    classes, width = c_buf.shape
    per = tile // LANES
    groups = classes // tile
    blocks = off_ref.shape[1] // 2
    rows = x_ref.shape[0] // chunks
    used = off_ref[0, 2 * blocks - 1]

    def span(g):
        return pl.ds(pl.multiple_of(g * tile, tile), tile)

    def ins(g):
        at = span(g)
        return (
            pltpu.make_async_copy(c_hbm.at[at], c_buf.at[at], c_sem.at[g]),
            pltpu.make_async_copy(m_hbm.at[at], m_buf.at[at], m_sem.at[g]),
        )

    def outs(g):
        at, slot = span(g), lax.bitwise_and(g, 1)
        return (
            pltpu.make_async_copy(c_new.at[slot], co_hbm.at[at], co_sem.at[slot]),
            pltpu.make_async_copy(m_new.at[slot], mo_hbm.at[at], mo_sem.at[slot]),
        )

    def fetch(start):
        slot = lax.bitwise_and(lax.shift_right_logical(start, step.bit_length() - 1), 1)
        at = pl.ds(pl.multiple_of(start, step), step)
        return slot, pltpu.make_async_copy(w_hbm.at[at], buf.at[slot], w_sem.at[slot])

    @pl.when(used > 0)
    def _():
        fetch(0)[1].start()

    for g in range(groups):
        for copy in ins(g):
            copy.start()
    for j in range(chunks):
        den = d_refs[0][j]
        for q in range(1, chunks):
            den = den + d_refs[q][j ^ q]
        rate = logit_scale / den
        rate_ref[j] = rate.astype(bf16)
        if j == 0:
            scale_ref[...] = rate

    def work(done, size):
        slot = lax.bitwise_and(lax.shift_right_logical(done, step.bit_length() - 1), 1)
        at = pl.ds(pl.multiple_of(done, step), size)
        exact = min(size, 256)
        ids = iota((exact, rows), 0).astype(f32).astype(bf16)
        lines = []
        for h in range(0, size, exact):
            parts = []
            for j in range(chunks):
                place = at_ref[j] - (done + h)
                place = jnp.where((place >= 0) & (place < exact), place, -1).astype(f32).astype(bf16)
                g = buf[slot, h : h + exact, j * rows : (j + 1) * rows] * rate_ref[j]
                parts.append(jnp.where(ids == place, g - jnp.asarray(logit_scale, bf16), g))
            lines.append(jnp.concatenate(parts, axis=1))
        dw = dot(jnp.concatenate(lines, axis=0), x_ref[...], 1, 0)
        c = raw_ref[at, :].astype(f32)
        inv = 1.0 / jnp.sqrt(jnp.sum(c * c, axis=1, keepdims=True) + eps)
        along = jnp.sum(c * dw, axis=1, keepdims=True) * (inv * inv)
        dw_ref[at, :] = ((dw - c * along) * (inv * (1.0 / sharpness))).astype(bf16)
        dw_ref[pl.ds(pl.multiple_of(done + size, size), 2 * LANES), :] = jnp.zeros((2 * LANES, width), bf16)

    def one(done):
        @pl.when(done + step < used)
        def _():
            fetch(done + step)[1].start()

        fetch(done)[1].wait()

        @pl.when(used - done > step // 2)
        def _():
            work(done, step)

        @pl.when(used - done <= step // 2)
        def _():
            work(done, step // 2)

        return done + step

    def group(g, done):
        done = lax.while_loop(lambda d: d < off_ref[0, blocks + (g + 1) * per - 1], one, done)
        for copy in ins(g):
            copy.wait()
        slot = lax.bitwise_and(g, 1)

        @pl.when(g >= 2)
        def _():
            for copy in outs(g - 2):
                copy.wait()

        lane = iota((LANES, LANES), 1)
        for k in range(per):
            base = pl.multiple_of(lax.shift_left(lax.shift_right_logical(off_ref[0, g * per + k], 4), 4), 16)
            mine = pl.ds(pl.multiple_of(g * tile + k * LANES, LANES), LANES)
            to = slice(k * LANES, (k + 1) * LANES)
            place = rep_ref[mine, :] - base
            place = jnp.concatenate([ones_where(place == lane), ones_where(place == lane + LANES)], axis=1)
            dw = dot(place, dw_ref[pl.ds(base, 2 * LANES), :], 1, 0)
            c = c_buf[mine, :].astype(f32)
            m = momentum_rate * m_buf[mine, :] + dw + weight_decay * c
            m_new[slot, to, :] = m
            c_new[slot, to, :] = (c - learn_rate * m).astype(bf16)
        for copy in outs(g):
            copy.start()
        return done

    @pl.when(used == 0)
    def _():
        dw_ref[: 2 * LANES, :] = jnp.zeros((2 * LANES, width), bf16)

    lax.fori_loop(0, groups, group, 0)
    for g in range(max(0, groups - 2), groups):
        for copy in outs(g):
            copy.wait()


def update(off, at, rep, raw, centres, momentum, w, x, dens, tile, step):
    chunks = len(dens)
    classes, width = centres.shape
    rows = x.shape[0] // chunks
    vm = pl.BlockSpec(memory_space=pltpu.VMEM)
    sems = pltpu.SemaphoreType.DMA((classes // tile,))
    return pl.pallas_call(
        lambda *refs: update_kernel(chunks, step, tile, *refs),
        in_specs=[pl.BlockSpec(memory_space=pltpu.SMEM), vm, vm, vm, HBM, HBM, HBM] + [vm] * (1 + chunks),
        out_specs=(HBM, HBM, vm),
        out_shape=(
            jax.ShapeDtypeStruct((classes, width), f32),
            jax.ShapeDtypeStruct((classes, width), bf16),
            jax.ShapeDtypeStruct((1, rows), f32),
        ),
        scratch_shapes=[
            pltpu.VMEM((chunks, 1, rows), bf16),
            pltpu.VMEM((classes + 2 * LANES + step, width), bf16),
            pltpu.VMEM((classes, width), bf16),
            pltpu.VMEM((classes, width), f32),
            pltpu.VMEM((2, tile, width), bf16),
            pltpu.VMEM((2, tile, width), f32),
            pltpu.VMEM((2, step, chunks * rows), bf16),
            pltpu.SemaphoreType.DMA((2,)),
            sems,
            sems,
            pltpu.SemaphoreType.DMA((2,)),
            pltpu.SemaphoreType.DMA((2,)),
        ],
        compiler_params=params(22 + 3 * chunks),
        cost_estimate=pl.CostEstimate(
            flops=rows * chunks * classes * width,
            bytes_accessed=rows * chunks * classes + 12 * classes * width,
            transcendentals=0,
        ),
        name="update",
    )(off, at, rep, raw, centres, momentum, w, x, *dens)


def body(embeddings, labels, centres, momentum, sample_home, sample_row):
    shards = lax.axis_size("cls")
    group = lax.axis_size("dp")
    chips = shards // 2
    home_rows, _ = centres.shape
    rows_here = embeddings.shape[0]
    here = sample_row.shape[0]
    classes, sampled = shards * home_rows, shards * here
    shard = lax.axis_index("cls")

    dims = (home_rows, rows_here, here, classes, sampled)
    told = tell(embeddings, sample_home, sample_row, labels, dims)

    from_z = [shift(told, "dp", m) for m in (1, group - 1)] + [shift(told, "dp", m) for m in range(2, group - 1)]
    early = jnp.stack([told] + [swap(told, "cls", 2 * q) for q in range(1, chips)])
    early_away = swap(early, "cls", 1)
    late0 = jnp.stack([z[:rows_here] for z in from_z])
    late = [late0] + [swap(late0, "cls", 2 * q) for q in range(1, chips)]
    late_away = []
    for x in late:
        late_away.append(swap(x, "cls", 1))

    me = shard.astype(jnp.int32).reshape(1)
    in_hbm = lambda x: pltpu.with_memory_space_constraint(x, pltpu.HBM)
    row, rep, cnt, off, known, table = prepare(me, early, early_away, dims)
    what, raw, num = pack(off, row, cnt, in_hbm(centres), min(1024, home_rows))
    at = label_places(me, known, table, [told] + from_z, chips, dims)
    tile = min(512, home_rows)
    w, own_den, turned, x = logits(off, early, early_away, late, late_away, what, num, at, tile, home_rows)
    w = in_hbm(w)

    den = own_den + swap(turned, "cls", 1)
    dens = [den] + [swap(den, "cls", 2 * q) for q in range(1, chips)]

    self_part, away_part = row_parts(off, what, at, w, 2 * rows_here, tile)
    pair = self_part.astype(f32) + swap(away_part, "cls", 1).astype(f32)
    sums = [swap(pair[q].astype(bf16), "cls", 2 * q) for q in range(1, chips)]

    momentum_new, centres_new, scale = update(
        off, at, rep, raw, in_hbm(centres), in_hbm(momentum), w, x, dens, min(512, home_rows), 512
    )
    total = pair[0]
    for got in sums:
        total = total + got.astype(f32)
    xfloat = embeddings.astype(f32)
    row_norm = jnp.sqrt(jnp.sum(xfloat * xfloat, axis=1, keepdims=True) + eps)
    unit = xfloat / row_norm
    scale = scale[0, :rows_here][:, None]
    dunit = total[:rows_here] * scale - logit_scale * total[rows_here:]
    emb_grad = (dunit - unit * jnp.sum(unit * dunit, axis=1, keepdims=True)) / row_norm
    return (emb_grad, momentum_new, centres_new)


def solution(mesh):
    placed = (
        P(("dp", "cls"), None),
        P("dp"),
        P("cls", None),
        P("cls", None),
        P("cls", None),
        P("cls"),
    )
    return jax.shard_map(
        body,
        mesh=mesh,
        in_specs=placed,
        out_specs=(P(("dp", "cls"), None), P("cls", None), P("cls", None)),
        check_vma=False,
    )
```

```python
import math

import jax
import jax.numpy as jnp
from jax import lax
from jax.experimental import pallas as pl
from jax.experimental.pallas import tpu as pltpu
from jax.sharding import PartitionSpec as P

eps = 1e-06
logit_scale = 64.0
margin = 0.35
momentum_rate = 0.9
learn_rate = 0.1
weight_decay = 0.0005

LANES = 128
OUT = 4
sharpness = logit_scale * math.log2(math.e)
HBM = pl.BlockSpec(memory_space=pltpu.HBM)
bf16 = jnp.bfloat16
f32 = jnp.float32


def dot(a, b, ca, cb):
    return lax.dot_general(a, b, (((ca,), (cb,)), ((), ())), preferred_element_type=f32)


def swap(x, axis_name, m):
    n = lax.axis_size(axis_name)
    return lax.ppermute(x, axis_name, [(i, i ^ m) for i in range(n)])


def shift(x, axis_name, m):
    n = lax.axis_size(axis_name)
    return lax.ppermute(x, axis_name, [(i, (i + m) % n) for i in range(n)])


def params(mib):
    return pltpu.CompilerParams(vmem_limit_bytes=mib << 20)


def iota(shape, axis):
    return lax.broadcasted_iota(jnp.int32, shape, axis)


def ones_where(mask):
    return mask.astype(f32).astype(bf16)


def look_up(table, hi, lo, limit):
    n_hi, n = table.shape[0], hi.shape[1]
    oh = ones_where(iota((n_hi, n), 0) == hi)
    got = jnp.zeros((LANES, n), f32)
    for bits in range(0, 8 * pieces_of(limit), 8):
        piece = lax.bitwise_and(lax.shift_right_logical(table, bits), 255).astype(f32).astype(bf16)
        got = got + float(1 << bits) * dot(piece, oh, 0, 0)
    pick = jnp.where(iota((LANES, n), 0) == lo, got, 0.0)
    return jnp.sum(pick, axis=0, keepdims=True).astype(jnp.int32)


def pieces_of(limit):
    return -(-(limit - 1).bit_length() // 8)


def tell_kernel(dims, x_ref, home_ref, row_ref, lab_ref, o_ref):
    home_rows, rows_here, _, classes, sampled = dims
    width = x_ref.shape[1]
    x = x_ref[...].astype(f32)
    scale = sharpness / jnp.sqrt(jnp.sum(x * x, axis=1, keepdims=True) + eps)
    o_ref[:rows_here, :] = (x * scale).astype(bf16)
    per = width // LANES
    lines = []
    for values, limit in ((home_ref[...] * home_rows + row_ref[...], classes), (lab_ref[...], sampled)):
        for k in range(pieces_of(limit)):
            v = lax.bitwise_and(lax.shift_right_logical(values, 8 * k), 255).astype(f32)
            for r in range(v.shape[0] // per):
                lines.append(jnp.concatenate([v[r * per + c : r * per + c + 1, :] for c in range(per)], axis=1))
    lines += [jnp.zeros_like(lines[0])] * (o_ref.shape[0] - rows_here - len(lines))
    o_ref[rows_here:, :] = jnp.concatenate(lines, axis=0).astype(bf16)


def tell(embeddings, home, row, labels, dims):
    _, rows_here, _, classes, sampled = dims
    width = embeddings.shape[1]
    lines = (row.size * pieces_of(classes) + labels.size * pieces_of(sampled)) // width
    args = [embeddings, home.reshape(-1, LANES), row.reshape(-1, LANES), labels.reshape(-1, LANES)]
    args = [pltpu.with_memory_space_constraint(x, pltpu.HBM) for x in args]
    return pl.pallas_call(
        lambda *refs: tell_kernel(dims, *refs),
        out_shape=jax.ShapeDtypeStruct((-(-(rows_here + lines) // 16) * 16, width), bf16),
        compiler_params=params(4),
        name="tell",
    )(*args)


def decode(get, row, count, number):
    total = get(row, row + count).astype(f32)
    for k in range(1, number):
        total = total + float(1 << (8 * k)) * get(row + k * count, row + (k + 1) * count).astype(f32)
    return total


def swap_groups(x, size):
    n = x.shape[1] // size
    return jnp.concatenate([x[:, (g ^ 1) * size : ((g ^ 1) + 1) * size] for g in range(n)], axis=1)


def prep_kernel(dims, shard_ref, mine_ref, away_ref, row_ref, rep_ref, cnt_ref, off_ref, known_ref, table_ref):
    home_rows, rows_here, here, classes, _ = dims
    base = shard_ref[0] * home_rows
    chips, _, width = mine_ref.shape
    blocks = home_rows // LANES
    lines, id_bytes = here // width, pieces_of(classes)
    total = jnp.zeros((LANES, blocks), f32)
    total_t = jnp.zeros((blocks, LANES), f32)
    for tile in range(2 * chips):
        ref = (mine_ref, away_ref)[tile % 2]
        ids = decode(lambda p, q: ref[tile // 2, p:q, :], rows_here, lines, id_bytes).astype(jnp.int32)
        h = ids - base
        for k in range(lines):
            a = ones_where(iota((blocks, width), 0) == lax.shift_right_arithmetic(h[k : k + 1], 7))
            b = ones_where(iota((LANES, width), 0) == lax.bitwise_and(h[k : k + 1], LANES - 1))
            total = total + dot(b, a, 1, 1)
            total_t = total_t + dot(a, b, 1, 1)
            for c in range(width // LANES):
                to = (tile * lines + k) * (width // LANES) + c
                table_ref[to : to + 1, :] = ids[k : k + 1, c * LANES : (c + 1) * LANES]
    have, have_t = ones_where(total > 0), ones_where(total_t > 0)
    before = ones_where(iota((LANES, LANES), 1) < iota((LANES, LANES), 0))
    ahead = ones_where(iota((LANES, LANES), 0) < iota((LANES, LANES), 1))
    ahead_b = ones_where(iota((blocks, blocks), 0) < iota((blocks, blocks), 1))
    before_b = ones_where(iota((blocks, blocks), 1) < iota((blocks, blocks), 0))
    sizes = jnp.broadcast_to(jnp.sum(have.astype(f32), axis=0, keepdims=True), (8, blocks))
    start = dot(sizes.astype(bf16), ahead_b, 1, 0)
    off_ref[...] = jnp.concatenate([start, start + sizes], axis=1).astype(jnp.int32)
    sizes_t = jnp.broadcast_to(jnp.sum(have_t.astype(f32), axis=1, keepdims=True), (blocks, LANES))
    start_t = dot(before_b, sizes_t.astype(bf16), 1, 0)
    pos = jnp.where(total > 0, dot(before, have, 1, 0) + start[:1], -1.0).astype(jnp.int32)
    pos_t = jnp.where(total_t > 0, dot(have_t, ahead, 1, 0) + start_t, -1.0).astype(jnp.int32)
    for k in range(blocks):
        rows = slice(k * LANES, (k + 1) * LANES)
        row_ref[k] = pos_t[k : k + 1, :]
        rep_ref[rows, :] = jnp.broadcast_to(pos[:, k : k + 1], (LANES, LANES))
        cnt_ref[rows, :] = jnp.broadcast_to(total[:, k : k + 1], (LANES, LANES))
    known_ref[...] = jnp.maximum(pos_t, 0)


def labels_kernel(dims, shard_ref, known_ref, table_ref, *refs):
    home_rows, rows_here, here, classes, sampled = dims
    z_refs, at_ref = refs[:-1], refs[-1]
    chips = at_ref.shape[0]
    width = z_refs[0].shape[1]
    shard = shard_ref[0]
    base = shard * home_rows
    lines, id_bytes = here // width, pieces_of(classes)
    known = known_ref[...]
    table = table_ref[...]
    own = 2 * rows_here
    group_rows = 2 * chips * rows_here
    lab_lines, lab_bytes = group_rows // width, pieces_of(sampled)
    per_tile = here // LANES
    for z, ref in enumerate(z_refs):
        first = rows_here + lines * id_bytes
        got = decode(lambda p, q: ref[p:q, :], first, lab_lines, lab_bytes)
        lab = jnp.concatenate([got[k : k + 1] for k in range(lab_lines)], axis=1)
        bit = 1
        while bit < 2 * chips:
            lab = jnp.where(lax.bitwise_and(shard, bit) != 0, swap_groups(lab, bit * rows_here), lab)
            bit *= 2
        lab = lab.astype(jnp.int32)
        tile = lax.bitwise_xor(lax.shift_right_logical(lab, here.bit_length() - 1), shard)
        hi = tile * per_tile + lax.shift_right_logical(lax.bitwise_and(lab, here - 1), 7)
        h = look_up(table, hi, lax.bitwise_and(lab, LANES - 1), classes) - base
        at = look_up(known, lax.shift_right_arithmetic(h, 7), lax.bitwise_and(h, LANES - 1), home_rows)
        at = jnp.where((h >= 0) & (h < home_rows), at, -1)
        for j in range(chips):
            at_ref[j, :, z * own : (z + 1) * own] = at[:, j * own : (j + 1) * own]


def prepare(shard, mine, away, dims):
    home_rows, _, _, _, sampled = dims
    vm = pl.BlockSpec(memory_space=pltpu.VMEM)
    blocks = home_rows // LANES
    i32 = jnp.int32
    return pl.pallas_call(
        lambda *refs: prep_kernel(dims, *refs),
        in_specs=[pl.BlockSpec(memory_space=pltpu.SMEM), vm, vm],
        out_specs=(vm,) * 6,
        out_shape=(
            jax.ShapeDtypeStruct((blocks, 1, LANES), i32),
            jax.ShapeDtypeStruct((home_rows, LANES), i32),
            jax.ShapeDtypeStruct((home_rows, LANES), f32),
            jax.ShapeDtypeStruct((8, 2 * blocks), i32),
            jax.ShapeDtypeStruct((blocks, LANES), i32),
            jax.ShapeDtypeStruct((sampled // LANES, LANES), i32),
        ),
        compiler_params=params(10),
        cost_estimate=pl.CostEstimate(flops=128 * sampled * LANES, bytes_accessed=1024 * home_rows, transcendentals=0),
        name="prep",
    )(shard, mine, away)


def label_places(shard, known, table, told, chips, dims):
    rows_here = dims[1]
    vm = pl.BlockSpec(memory_space=pltpu.VMEM)
    return pl.pallas_call(
        lambda *refs: labels_kernel(dims, *refs),
        in_specs=[pl.BlockSpec(memory_space=pltpu.SMEM)] + [vm] * (2 + len(told)),
        out_specs=vm,
        out_shape=jax.ShapeDtypeStruct((chips, 1, 2 * len(told) * rows_here), jnp.int32),
        compiler_params=params(12),
        cost_estimate=pl.CostEstimate(
            flops=8 * table.size * 2 * chips * len(told) * rows_here, bytes_accessed=8 * table.size, transcendentals=0
        ),
        name="places",
    )(shard, known, table, *told)


WINDOW = LANES + 16


def pack_kernel(off_ref, row_ref, cnt_ref, c_ref, what_ref, raw_ref, num_ref):
    i = pl.program_id(0)

    @pl.when(i == 0)
    def _():
        for ref in (what_ref, raw_ref, num_ref):
            ref[:16, :] = jnp.zeros((16, ref.shape[1]), ref.dtype)

    c = c_ref[...].astype(f32)
    width = c.shape[1]
    unit = (c * (1.0 / jnp.sqrt(jnp.sum(c * c, axis=1, keepdims=True) + eps))).astype(bf16)
    cnt = cnt_ref[...]
    high = jnp.floor(cnt * (1.0 / 256.0))
    low = cnt - 256.0 * high
    here = row_ref.shape[0]
    todo = []
    for k in range(here):
        rows = slice(k * LANES, (k + 1) * LANES)
        base = pl.multiple_of(lax.shift_left(lax.shift_right_logical(off_ref[0, i * here + k], 4), 4), 16)
        pick = ones_where(iota((WINDOW, LANES), 0) + base == row_ref[k])
        right = jnp.concatenate([unit[rows], c_ref[rows, :], low[rows].astype(bf16), high[rows].astype(bf16)], axis=1)
        todo.append((base, dot(pick, right, 1, 0)))
    for base, got in todo:
        num = got[:, 2 * width : 2 * width + LANES] + 256.0 * got[:, 2 * width + LANES :]
        for ref, new in ((what_ref, got[:, :width]), (raw_ref, got[:, width : 2 * width]), (num_ref, num)):
            new = new.astype(ref.dtype)
            ref[pl.ds(base, 16), :] = ref[pl.ds(base, 16), :] + new[:16]
            ref[pl.ds(pl.multiple_of(base + 16, 16), LANES), :] = new[16:]

    @pl.when(i == pl.num_programs(0) - 1)
    def _():
        for ref in (what_ref, raw_ref, num_ref):
            ref[pl.ds(pl.multiple_of(base + WINDOW, 16), 4 * LANES), :] = jnp.zeros((4 * LANES, ref.shape[1]), ref.dtype)


def pack(off, row, cnt, centres, tile):
    classes, width = centres.shape
    per = tile // LANES
    room = classes + 6 * LANES
    whole = lambda n: pl.BlockSpec((room, n), lambda i: (0, 0))
    return pl.pallas_call(
        pack_kernel,
        grid=(classes // tile,),
        in_specs=[
            pl.BlockSpec(memory_space=pltpu.SMEM),
            pl.BlockSpec((per, 1, LANES), lambda i: (i, 0, 0)),
            pl.BlockSpec((tile, LANES), lambda i: (i, 0)),
            pl.BlockSpec((tile, width), lambda i: (i, 0)),
        ],
        out_specs=(whole(width), whole(width), whole(LANES)),
        out_shape=(
            jax.ShapeDtypeStruct((room, width), bf16),
            jax.ShapeDtypeStruct((room, width), bf16),
            jax.ShapeDtypeStruct((room, LANES), f32),
        ),
        compiler_params=params(20),
        cost_estimate=pl.CostEstimate(flops=5 * classes * LANES * width, bytes_accessed=4 * classes * width, transcendentals=0),
        name="pack",
    )(off, row, cnt, centres)


def tiles_used(off, tile):
    return lax.shift_right_logical(off[0, off.shape[1] - 1] + tile - 1, tile.bit_length() - 1)


def last_used(i, off, tile):
    return lax.max(lax.min(i, tiles_used(off, tile) - 1), 0)


def logits_kernel(chunks, tile, off_ref, e0_ref, e1_ref, what_ref, num_ref, at_ref, *refs):
    l0_refs, l1_refs = refs[:chunks], refs[chunks : 2 * chunks]
    w_hbm, den_ref, turn_ref, x_ref, d_acc, w_buf, w_sem = refs[2 * chunks :]
    group, rows_here, _ = l0_refs[0].shape
    rows = 2 * (group + 1) * rows_here
    for j in range(chunks):
        for r, (early, late) in enumerate(((e0_ref, l0_refs[j]), (e1_ref, l1_refs[j]))):
            to = j * rows + r * rows_here
            x_ref[to : to + rows_here, :] = early[j, :rows_here, :]
            for z in range(group):
                to = j * rows + (2 * z + 2 + r) * rows_here
                x_ref[to : to + rows_here, :] = late[z]
    d_acc[...] = jnp.zeros_like(d_acc)
    steps = tiles_used(off_ref, tile)
    half = tile // 2
    cut = rows

    def put(t):
        slot = lax.bitwise_and(t, 1)
        here = pl.ds(pl.multiple_of(t * tile, tile), tile)
        return pltpu.make_async_copy(w_buf.at[slot], w_hbm.at[here], w_sem.at[slot])

    def weigh(first, size, j, slot):
        here = pl.ds(pl.multiple_of(first, half), size)
        ids = iota((size, LANES), 0) + first
        num = num_ref[here, :]
        num_t = num + (math.exp(-logit_scale * margin) - 1.0)
        at = at_ref[j]
        for left in range(0, rows, cut):
            x = x_ref[pl.ds(pl.multiple_of(j * rows + left, cut), cut), :]
            cos = dot(what_ref[here, :], x, 1, 1)
            for k in range(0, cut, LANES):
                cols = slice(left + k, left + k + LANES)
                w = jnp.exp2(cos[:, k : k + LANES]) * jnp.where(ids == at[:, cols], num_t, num)
                d_acc[j, :, cols] += jnp.sum(w.reshape(size // 8, 8, LANES), axis=0)
                w_buf[slot, :size, pl.ds(pl.multiple_of(j * rows + left + k, LANES), LANES)] = w.astype(bf16)

    def one(t, size):
        @pl.when(t >= 2)
        def _():
            put(t - 2).wait()

        slot = lax.bitwise_and(t, 1)
        if size < tile:
            w_buf[slot, size:, :] = jnp.zeros((tile - size, w_buf.shape[2]), bf16)

        together = math.gcd(chunks, 4)

        def chunk(j, carry):
            for k in range(together):
                weigh(t * tile, size, j * together + k, slot)
            return carry

        lax.fori_loop(0, chunks // together, chunk, 0)
        put(t).start()

    def full(t, carry):
        one(t, tile)
        return carry

    used = off_ref[0, off_ref.shape[1] - 1]
    whole = lax.shift_right_logical(used + half - 1, tile.bit_length() - 1)
    lax.fori_loop(0, whole, full, 0)

    @pl.when(whole < steps)
    def _():
        one(whole, half)

    for back in (2, 1):

        @pl.when(steps >= back)
        def _():
            put(steps - back).wait()

    for j in range(chunks):
        den = jnp.sum(d_acc[j], axis=0, keepdims=True)
        den_ref[j] = den
        turn_ref[j] = swap_groups(den, rows_here)


def logits(off, early0, early1, late0, late1, what, num, at, tile, classes):
    chunks = len(late0)
    group, rows_here, width = late0[0].shape
    rows = 2 * (group + 1) * rows_here
    vm = pl.BlockSpec(memory_space=pltpu.VMEM)
    return pl.pallas_call(
        lambda *refs: logits_kernel(chunks, tile, *refs),
        in_specs=[pl.BlockSpec(memory_space=pltpu.SMEM)] + [vm] * (5 + 2 * chunks),
        out_specs=(HBM, vm, vm, vm),
        out_shape=(
            pltpu.HBM((classes, chunks * rows), bf16),
            jax.ShapeDtypeStruct((chunks, 1, rows), f32),
            jax.ShapeDtypeStruct((chunks, 1, rows), f32),
            jax.ShapeDtypeStruct((chunks * rows, width), bf16),
        ),
        scratch_shapes=[
            pltpu.VMEM((chunks, 8, rows), f32),
            pltpu.VMEM((2, tile, chunks * rows), bf16),
            pltpu.SemaphoreType.DMA((2,)),
        ],
        compiler_params=params(8 + 3 * chunks // 2),
        cost_estimate=pl.CostEstimate(
            flops=chunks * rows * classes * width,
            bytes_accessed=chunks * rows * classes + classes * width,
            transcendentals=chunks * rows * classes // 2,
        ),
        name="logits",
    )(off, early0, early1, what, num, at, *late0, *late1)


def own_columns(tile, own, at):
    return pl.BlockSpec((tile, own), lambda i, off: (last_used(i, off, tile), at))


def rows_kernel(chunks, off_ref, what_ref, at_ref, *refs):
    w_refs, (self_ref, away_ref), acc = refs[:chunks], refs[chunks : chunks + 2], refs[chunks + 2]
    i = pl.program_id(0)
    tile = what_ref.shape[0]
    own = w_refs[0].shape[1]
    half = own // 2

    @pl.when(i == 0)
    def _():
        acc[...] = jnp.zeros_like(acc)

    left = off_ref[0, off_ref.shape[1] - 1] - i * tile

    def add(size):
        ids = iota((size, own), 0) + i * tile
        a = [w[:size, :] for w in w_refs] + [ones_where(ids == at_ref[j][:, :own]) for j in range(chunks)]
        acc[...] += dot(jnp.concatenate(a, axis=1), what_ref[:size, :], 0, 0)

    @pl.when(left > tile // 2)
    def _():
        add(tile)

    @pl.when((left > 0) & (left <= tile // 2))
    def _():
        add(tile // 2)

    @pl.when(i == pl.num_programs(0) - 1)
    def _():
        for j in range(chunks):
            for part in range(2):
                at = (part * chunks + j) * own
                self_ref[j, part * half : (part + 1) * half, :] = acc[at : at + half, :].astype(bf16)
                away_ref[j, part * half : (part + 1) * half, :] = acc[at + half : at + own, :].astype(bf16)


def row_parts(off, what, at, w, own, tile):
    chunks, _, rows = at.shape
    width = what.shape[1]
    out = jax.ShapeDtypeStruct((chunks, own, width), bf16)
    whole = pl.BlockSpec((chunks, own, width), lambda i, n: (0, 0, 0))
    return pl.pallas_call(
        lambda *refs: rows_kernel(chunks, *refs),
        grid_spec=pltpu.PrefetchScalarGridSpec(
            num_scalar_prefetch=1,
            grid=(w.shape[0] // tile,),
            in_specs=[
                pl.BlockSpec((tile, width), lambda i, off: (last_used(i, off, tile), 0)),
                pl.BlockSpec(at.shape, lambda i, n: (0, 0, 0)),
            ]
            + [own_columns(tile, own, j * rows // own) for j in range(chunks)],
            out_specs=(whole, whole),
            scratch_shapes=[pltpu.VMEM((2 * chunks * own, width), f32)],
        ),
        out_shape=(out, out),
        compiler_params=params(8 + 3 * chunks),
        cost_estimate=pl.CostEstimate(
            flops=2 * chunks * own * w.shape[0] * width, bytes_accessed=2 * what.size, transcendentals=0
        ),
        name="rows",
    )(off, what, at, *[w] * chunks)


def update_kernel(chunks, step, tile, off_ref, at_ref, rep_ref, raw_ref, c_hbm, m_hbm, *refs):
    w_hbm, x_ref, d_refs = refs[0], refs[1], refs[2 : 2 + chunks]
    mo_hbm, co_hbm, scale_ref, rate_ref, dw_ref, c_buf, m_buf, c_new, m_new, buf, w_sem, c_sem, m_sem, co_sem, mo_sem = refs[2 + chunks :]
    classes, width = c_buf.shape
    per = tile // LANES
    groups = classes // tile
    blocks = off_ref.shape[1] // 2
    rows = x_ref.shape[0] // chunks
    used = off_ref[0, 2 * blocks - 1]

    def span(g):
        return pl.ds(pl.multiple_of(g * tile, tile), tile)

    def ins(g):
        at = span(g)
        return (
            pltpu.make_async_copy(c_hbm.at[at], c_buf.at[at], c_sem.at[g]),
            pltpu.make_async_copy(m_hbm.at[at], m_buf.at[at], m_sem.at[g]),
        )

    def outs(g):
        at, slot = span(g), lax.bitwise_and(g, OUT - 1)
        return (
            pltpu.make_async_copy(c_new.at[slot], co_hbm.at[at], co_sem.at[slot]),
            pltpu.make_async_copy(m_new.at[slot], mo_hbm.at[at], mo_sem.at[slot]),
        )

    def fetch(start):
        slot = lax.bitwise_and(lax.shift_right_logical(start, step.bit_length() - 1), 1)
        at = pl.ds(pl.multiple_of(start, step), step)
        return slot, pltpu.make_async_copy(w_hbm.at[at], buf.at[slot], w_sem.at[slot])

    for first in (0, step):

        @pl.when(used > first)
        def _():
            fetch(first)[1].start()

    for g in range(groups):
        for copy in ins(g):
            copy.start()
    for j in range(chunks):
        den = d_refs[0][j]
        for q in range(1, chunks):
            den = den + d_refs[q][j ^ q]
        rate = logit_scale / den
        rate_ref[j] = rate.astype(bf16)
        if j == 0:
            scale_ref[...] = rate

    def work(done, size):
        slot = lax.bitwise_and(lax.shift_right_logical(done, step.bit_length() - 1), 1)
        at = pl.ds(pl.multiple_of(done, step), size)
        exact = min(size, 256)
        ids = iota((exact, rows), 0).astype(f32).astype(bf16)
        lines = []
        for h in range(0, size, exact):
            parts = []
            for j in range(chunks):
                place = at_ref[j] - (done + h)
                place = jnp.where((place >= 0) & (place < exact), place, -1).astype(f32).astype(bf16)
                g = buf[slot, h : h + exact, j * rows : (j + 1) * rows] * rate_ref[j]
                parts.append(jnp.where(ids == place, g - jnp.asarray(logit_scale, bf16), g))
            lines.append(jnp.concatenate(parts, axis=1))
        dw = dot(jnp.concatenate(lines, axis=0), x_ref[...], 1, 0)
        c = raw_ref[at, :].astype(f32)
        inv = 1.0 / jnp.sqrt(jnp.sum(c * c, axis=1, keepdims=True) + eps)
        along = jnp.sum(c * dw, axis=1, keepdims=True) * (inv * inv)
        dw_ref[at, :] = ((dw - c * along) * (inv * (1.0 / sharpness))).astype(bf16)
        dw_ref[pl.ds(pl.multiple_of(done + size, size), 2 * LANES), :] = jnp.zeros((2 * LANES, width), bf16)

    def one(done):
        fetch(done)[1].wait()

        @pl.when(used - done > step // 2)
        def _():
            work(done, step)

        @pl.when(used - done <= step // 2)
        def _():
            work(done, step // 2)

        @pl.when(done + 2 * step < used)
        def _():
            fetch(done + 2 * step)[1].start()

        return done + step

    def group(g, done):
        done = lax.while_loop(lambda d: d < off_ref[0, blocks + (g + 1) * per - 1], one, done)
        for copy in ins(g):
            copy.wait()
        slot = lax.bitwise_and(g, OUT - 1)

        @pl.when(g >= OUT)
        def _():
            for copy in outs(g - OUT):
                copy.wait()

        lane = iota((LANES, LANES), 1)
        for k in range(per):
            base = pl.multiple_of(lax.shift_left(lax.shift_right_logical(off_ref[0, g * per + k], 4), 4), 16)
            mine = pl.ds(pl.multiple_of(g * tile + k * LANES, LANES), LANES)
            to = slice(k * LANES, (k + 1) * LANES)
            place = rep_ref[mine, :] - base
            place = jnp.concatenate([ones_where(place == lane), ones_where(place == lane + LANES)], axis=1)
            dw = dot(place, dw_ref[pl.ds(base, 2 * LANES), :], 1, 0)
            c = c_buf[mine, :].astype(f32)
            m = momentum_rate * m_buf[mine, :] + dw + weight_decay * c
            m_new[slot, to, :] = m
            c_new[slot, to, :] = (c - learn_rate * m).astype(bf16)
        for copy in outs(g):
            copy.start()
        return done

    @pl.when(used == 0)
    def _():
        dw_ref[: 2 * LANES, :] = jnp.zeros((2 * LANES, width), bf16)

    lax.fori_loop(0, groups, group, 0)
    for g in range(max(0, groups - OUT), groups):
        for copy in outs(g):
            copy.wait()


def update(off, at, rep, raw, centres, momentum, w, x, dens, tile, step):
    chunks = len(dens)
    classes, width = centres.shape
    rows = x.shape[0] // chunks
    vm = pl.BlockSpec(memory_space=pltpu.VMEM)
    sems = pltpu.SemaphoreType.DMA((classes // tile,))
    return pl.pallas_call(
        lambda *refs: update_kernel(chunks, step, tile, *refs),
        in_specs=[pl.BlockSpec(memory_space=pltpu.SMEM), vm, vm, vm, HBM, HBM, HBM] + [vm] * (1 + chunks),
        out_specs=(HBM, HBM, vm),
        out_shape=(
            jax.ShapeDtypeStruct((classes, width), f32),
            jax.ShapeDtypeStruct((classes, width), bf16),
            jax.ShapeDtypeStruct((1, rows), f32),
        ),
        scratch_shapes=[
            pltpu.VMEM((chunks, 1, rows), bf16),
            pltpu.VMEM((classes + 2 * LANES + step, width), bf16),
            pltpu.VMEM((classes, width), bf16),
            pltpu.VMEM((classes, width), f32),
            pltpu.VMEM((OUT, tile, width), bf16),
            pltpu.VMEM((OUT, tile, width), f32),
            pltpu.VMEM((2, step, chunks * rows), bf16),
            pltpu.SemaphoreType.DMA((2,)),
            sems,
            sems,
            pltpu.SemaphoreType.DMA((OUT,)),
            pltpu.SemaphoreType.DMA((OUT,)),
        ],
        compiler_params=params(22 + 3 * chunks),
        cost_estimate=pl.CostEstimate(
            flops=rows * chunks * classes * width,
            bytes_accessed=rows * chunks * classes + 12 * classes * width,
            transcendentals=0,
        ),
        name="update",
    )(off, at, rep, raw, centres, momentum, w, x, *dens)


def body(embeddings, labels, centres, momentum, sample_home, sample_row):
    shards = lax.axis_size("cls")
    group = lax.axis_size("dp")
    chips = shards // 2
    home_rows, _ = centres.shape
    rows_here = embeddings.shape[0]
    here = sample_row.shape[0]
    classes, sampled = shards * home_rows, shards * here
    shard = lax.axis_index("cls")

    dims = (home_rows, rows_here, here, classes, sampled)
    told = tell(embeddings, sample_home, sample_row, labels, dims)

    from_z = []
    for m in [1, group - 1] + list(range(2, group - 1)):
        from_z.append(shift(told, "dp", m))
    early = jnp.stack([told] + [swap(told, "cls", 2 * q) for q in range(1, chips)])
    early_away = swap(early, "cls", 1)
    late0 = jnp.stack([z[:rows_here] for z in from_z])
    late = [late0]
    for q in range(1, chips):
        late.append(swap(late0, "cls", 2 * q))
    late_away = []
    for x in late:
        late_away.append(swap(x, "cls", 1))

    me = shard.astype(jnp.int32).reshape(1)
    in_hbm = lambda x: pltpu.with_memory_space_constraint(x, pltpu.HBM)
    row, rep, cnt, off, known, table = prepare(me, early, early_away, dims)
    what, raw, num = pack(off, row, cnt, in_hbm(centres), min(1024, home_rows))
    at = label_places(me, known, table, [told] + from_z, chips, dims)
    tile = min(512, home_rows)
    w, own_den, turned, x = logits(off, early, early_away, late, late_away, what, num, at, tile, home_rows)
    w = in_hbm(w)

    den = own_den + swap(turned, "cls", 1)
    dens = [den] + [swap(den, "cls", 2 * q) for q in range(1, chips)]

    self_part, away_part = row_parts(off, what, at, w, 2 * rows_here, tile)
    pair = self_part.astype(f32) + swap(away_part, "cls", 1).astype(f32)
    sums = [swap(pair[q].astype(bf16), "cls", 2 * q) for q in range(1, chips)]

    momentum_new, centres_new, scale = update(
        off, at, rep, raw, in_hbm(centres), in_hbm(momentum), w, x, dens, min(512, home_rows), 512
    )
    total = pair[0]
    for got in sums:
        total = total + got.astype(f32)
    xfloat = embeddings.astype(f32)
    row_norm = jnp.sqrt(jnp.sum(xfloat * xfloat, axis=1, keepdims=True) + eps)
    unit = xfloat / row_norm
    scale = scale[0, :rows_here][:, None]
    dunit = total[:rows_here] * scale - logit_scale * total[rows_here:]
    emb_grad = (dunit - unit * jnp.sum(unit * dunit, axis=1, keepdims=True)) / row_norm
    return (emb_grad, momentum_new, centres_new)


def solution(mesh):
    placed = (
        P(("dp", "cls"), None),
        P("dp"),
        P("cls", None),
        P("cls", None),
        P("cls", None),
        P("cls"),
    )
    return jax.shard_map(
        body,
        mesh=mesh,
        in_specs=placed,
        out_specs=(P(("dp", "cls"), None), P("cls", None), P("cls", None)),
        check_vma=False,
    )
```

```python
import math

import jax
import jax.numpy as jnp
from jax import lax
from jax.experimental import pallas as pl
from jax.experimental.pallas import tpu as pltpu
from jax.sharding import PartitionSpec as P

eps = 1e-06
logit_scale = 64.0
margin = 0.35
momentum_rate = 0.9
learn_rate = 0.1
weight_decay = 0.0005

LANES = 128
OUT = 4
sharpness = logit_scale * math.log2(math.e)
HBM = pl.BlockSpec(memory_space=pltpu.HBM)
bf16 = jnp.bfloat16
f32 = jnp.float32


def dot(a, b, ca, cb):
    return lax.dot_general(a, b, (((ca,), (cb,)), ((), ())), preferred_element_type=f32)


def swap(x, axis_name, m):
    n = lax.axis_size(axis_name)
    return lax.ppermute(x, axis_name, [(i, i ^ m) for i in range(n)])


def shift(x, axis_name, m):
    n = lax.axis_size(axis_name)
    return lax.ppermute(x, axis_name, [(i, (i + m) % n) for i in range(n)])


def params(mib):
    return pltpu.CompilerParams(vmem_limit_bytes=mib << 20)


def iota(shape, axis):
    return lax.broadcasted_iota(jnp.int32, shape, axis)


def ones_where(mask):
    return mask.astype(f32).astype(bf16)


def look_up(table, hi, lo, limit):
    n_hi, n = table.shape[0], hi.shape[1]
    oh = ones_where(iota((n_hi, n), 0) == hi)
    got = jnp.zeros((LANES, n), f32)
    for bits in range(0, 8 * pieces_of(limit), 8):
        piece = lax.bitwise_and(lax.shift_right_logical(table, bits), 255).astype(f32).astype(bf16)
        got = got + float(1 << bits) * dot(piece, oh, 0, 0)
    pick = jnp.where(iota((LANES, n), 0) == lo, got, 0.0)
    return jnp.sum(pick, axis=0, keepdims=True).astype(jnp.int32)


def pieces_of(limit):
    return -(-(limit - 1).bit_length() // 8)


def tell_kernel(dims, x_ref, home_ref, row_ref, lab_ref, o_ref):
    home_rows, rows_here, _, classes, sampled = dims
    width = x_ref.shape[1]
    x = x_ref[...].astype(f32)
    scale = sharpness / jnp.sqrt(jnp.sum(x * x, axis=1, keepdims=True) + eps)
    o_ref[:rows_here, :] = (x * scale).astype(bf16)
    per = width // LANES
    lines = []
    for values, limit in ((home_ref[...] * home_rows + row_ref[...], classes), (lab_ref[...], sampled)):
        for k in range(pieces_of(limit)):
            v = lax.bitwise_and(lax.shift_right_logical(values, 8 * k), 255).astype(f32)
            for r in range(v.shape[0] // per):
                lines.append(jnp.concatenate([v[r * per + c : r * per + c + 1, :] for c in range(per)], axis=1))
    lines += [jnp.zeros_like(lines[0])] * (o_ref.shape[0] - rows_here - len(lines))
    o_ref[rows_here:, :] = jnp.concatenate(lines, axis=0).astype(bf16)


def tell(embeddings, home, row, labels, dims):
    _, rows_here, _, classes, sampled = dims
    width = embeddings.shape[1]
    lines = (row.size * pieces_of(classes) + labels.size * pieces_of(sampled)) // width
    args = [embeddings, home.reshape(-1, LANES), row.reshape(-1, LANES), labels.reshape(-1, LANES)]
    args = [pltpu.with_memory_space_constraint(x, pltpu.HBM) for x in args]
    return pl.pallas_call(
        lambda *refs: tell_kernel(dims, *refs),
        out_shape=jax.ShapeDtypeStruct((-(-(rows_here + lines) // 16) * 16, width), bf16),
        compiler_params=params(4),
        name="tell",
    )(*args)


def decode(get, row, count, number):
    total = get(row, row + count).astype(f32)
    for k in range(1, number):
        total = total + float(1 << (8 * k)) * get(row + k * count, row + (k + 1) * count).astype(f32)
    return total


def swap_groups(x, size):
    n = x.shape[1] // size
    return jnp.concatenate([x[:, (g ^ 1) * size : ((g ^ 1) + 1) * size] for g in range(n)], axis=1)


def prep_kernel(dims, shard_ref, mine_ref, away_ref, row_ref, rep_ref, cnt_ref, off_ref, known_ref, table_ref):
    home_rows, rows_here, here, classes, _ = dims
    base = shard_ref[0] * home_rows
    chips, _, width = mine_ref.shape
    blocks = home_rows // LANES
    lines, id_bytes = here // width, pieces_of(classes)
    total = jnp.zeros((LANES, blocks), f32)
    total_t = jnp.zeros((blocks, LANES), f32)
    for tile in range(2 * chips):
        ref = (mine_ref, away_ref)[tile % 2]
        ids = decode(lambda p, q: ref[tile // 2, p:q, :], rows_here, lines, id_bytes).astype(jnp.int32)
        h = ids - base
        for k in range(lines):
            a = ones_where(iota((blocks, width), 0) == lax.shift_right_arithmetic(h[k : k + 1], 7))
            b = ones_where(iota((LANES, width), 0) == lax.bitwise_and(h[k : k + 1], LANES - 1))
            total = total + dot(b, a, 1, 1)
            total_t = total_t + dot(a, b, 1, 1)
            for c in range(width // LANES):
                to = (tile * lines + k) * (width // LANES) + c
                table_ref[to : to + 1, :] = ids[k : k + 1, c * LANES : (c + 1) * LANES]
    have, have_t = ones_where(total > 0), ones_where(total_t > 0)
    before = ones_where(iota((LANES, LANES), 1) < iota((LANES, LANES), 0))
    ahead = ones_where(iota((LANES, LANES), 0) < iota((LANES, LANES), 1))
    ahead_b = ones_where(iota((blocks, blocks), 0) < iota((blocks, blocks), 1))
    before_b = ones_where(iota((blocks, blocks), 1) < iota((blocks, blocks), 0))
    sizes = jnp.broadcast_to(jnp.sum(have.astype(f32), axis=0, keepdims=True), (8, blocks))
    start = dot(sizes.astype(bf16), ahead_b, 1, 0)
    off_ref[...] = jnp.concatenate([start, start + sizes], axis=1).astype(jnp.int32)
    sizes_t = jnp.broadcast_to(jnp.sum(have_t.astype(f32), axis=1, keepdims=True), (blocks, LANES))
    start_t = dot(before_b, sizes_t.astype(bf16), 1, 0)
    pos = jnp.where(total > 0, dot(before, have, 1, 0) + start[:1], -1.0).astype(jnp.int32)
    pos_t = jnp.where(total_t > 0, dot(have_t, ahead, 1, 0) + start_t, -1.0).astype(jnp.int32)
    for k in range(blocks):
        rows = slice(k * LANES, (k + 1) * LANES)
        row_ref[k] = pos_t[k : k + 1, :]
        rep_ref[rows, :] = jnp.broadcast_to(pos[:, k : k + 1], (LANES, LANES))
        cnt_ref[rows, :] = jnp.broadcast_to(total[:, k : k + 1], (LANES, LANES))
    known_ref[...] = jnp.maximum(pos_t, 0)


def labels_kernel(dims, shard_ref, known_ref, table_ref, *refs):
    home_rows, rows_here, here, classes, sampled = dims
    z_refs, at_ref = refs[:-1], refs[-1]
    chips = at_ref.shape[0]
    width = z_refs[0].shape[1]
    shard = shard_ref[0]
    base = shard * home_rows
    lines, id_bytes = here // width, pieces_of(classes)
    known = known_ref[...]
    table = table_ref[...]
    own = 2 * rows_here
    group_rows = 2 * chips * rows_here
    lab_lines, lab_bytes = group_rows // width, pieces_of(sampled)
    per_tile = here // LANES
    for z, ref in enumerate(z_refs):
        first = rows_here + lines * id_bytes
        got = decode(lambda p, q: ref[p:q, :], first, lab_lines, lab_bytes)
        lab = jnp.concatenate([got[k : k + 1] for k in range(lab_lines)], axis=1)
        bit = 1
        while bit < 2 * chips:
            lab = jnp.where(lax.bitwise_and(shard, bit) != 0, swap_groups(lab, bit * rows_here), lab)
            bit *= 2
        lab = lab.astype(jnp.int32)
        tile = lax.bitwise_xor(lax.shift_right_logical(lab, here.bit_length() - 1), shard)
        hi = tile * per_tile + lax.shift_right_logical(lax.bitwise_and(lab, here - 1), 7)
        h = look_up(table, hi, lax.bitwise_and(lab, LANES - 1), classes) - base
        at = look_up(known, lax.shift_right_arithmetic(h, 7), lax.bitwise_and(h, LANES - 1), home_rows)
        at = jnp.where((h >= 0) & (h < home_rows), at, -1)
        for j in range(chips):
            at_ref[j, :, z * own : (z + 1) * own] = at[:, j * own : (j + 1) * own]


def prepare(shard, mine, away, dims):
    home_rows, _, _, _, sampled = dims
    vm = pl.BlockSpec(memory_space=pltpu.VMEM)
    blocks = home_rows // LANES
    i32 = jnp.int32
    return pl.pallas_call(
        lambda *refs: prep_kernel(dims, *refs),
        in_specs=[pl.BlockSpec(memory_space=pltpu.SMEM), vm, vm],
        out_specs=(vm,) * 6,
        out_shape=(
            jax.ShapeDtypeStruct((blocks, 1, LANES), i32),
            jax.ShapeDtypeStruct((home_rows, LANES), i32),
            jax.ShapeDtypeStruct((home_rows, LANES), f32),
            jax.ShapeDtypeStruct((8, 2 * blocks), i32),
            jax.ShapeDtypeStruct((blocks, LANES), i32),
            jax.ShapeDtypeStruct((sampled // LANES, LANES), i32),
        ),
        compiler_params=params(10),
        cost_estimate=pl.CostEstimate(flops=128 * sampled * LANES, bytes_accessed=1024 * home_rows, transcendentals=0),
        name="prep",
    )(shard, mine, away)


def label_places(shard, known, table, told, chips, dims):
    rows_here = dims[1]
    vm = pl.BlockSpec(memory_space=pltpu.VMEM)
    return pl.pallas_call(
        lambda *refs: labels_kernel(dims, *refs),
        in_specs=[pl.BlockSpec(memory_space=pltpu.SMEM)] + [vm] * (2 + len(told)),
        out_specs=vm,
        out_shape=jax.ShapeDtypeStruct((chips, 1, 2 * len(told) * rows_here), jnp.int32),
        compiler_params=params(12),
        cost_estimate=pl.CostEstimate(
            flops=8 * table.size * 2 * chips * len(told) * rows_here, bytes_accessed=8 * table.size, transcendentals=0
        ),
        name="places",
    )(shard, known, table, *told)


WINDOW = LANES + 16


def pack_kernel(off_ref, row_ref, cnt_ref, c_ref, what_ref, raw_ref, num_ref):
    i = pl.program_id(0)

    @pl.when(i == 0)
    def _():
        for ref in (what_ref, raw_ref, num_ref):
            ref[:16, :] = jnp.zeros((16, ref.shape[1]), ref.dtype)

    c = c_ref[...].astype(f32)
    width = c.shape[1]
    unit = (c * (1.0 / jnp.sqrt(jnp.sum(c * c, axis=1, keepdims=True) + eps))).astype(bf16)
    cnt = cnt_ref[...]
    high = jnp.floor(cnt * (1.0 / 256.0))
    low = cnt - 256.0 * high
    here = row_ref.shape[0]
    todo = []
    for k in range(here):
        rows = slice(k * LANES, (k + 1) * LANES)
        base = pl.multiple_of(lax.shift_left(lax.shift_right_logical(off_ref[0, i * here + k], 4), 4), 16)
        pick = ones_where(iota((WINDOW, LANES), 0) + base == row_ref[k])
        right = jnp.concatenate([unit[rows], c_ref[rows, :], low[rows].astype(bf16), high[rows].astype(bf16)], axis=1)
        todo.append((base, dot(pick, right, 1, 0)))
    for base, got in todo:
        num = got[:, 2 * width : 2 * width + LANES] + 256.0 * got[:, 2 * width + LANES :]
        for ref, new in ((what_ref, got[:, :width]), (raw_ref, got[:, width : 2 * width]), (num_ref, num)):
            new = new.astype(ref.dtype)
            ref[pl.ds(base, 16), :] = ref[pl.ds(base, 16), :] + new[:16]
            ref[pl.ds(pl.multiple_of(base + 16, 16), LANES), :] = new[16:]

    @pl.when(i == pl.num_programs(0) - 1)
    def _():
        for ref in (what_ref, raw_ref, num_ref):
            ref[pl.ds(pl.multiple_of(base + WINDOW, 16), 4 * LANES), :] = jnp.zeros((4 * LANES, ref.shape[1]), ref.dtype)


def pack(off, row, cnt, centres, tile):
    classes, width = centres.shape
    per = tile // LANES
    room = classes + 6 * LANES
    whole = lambda n: pl.BlockSpec((room, n), lambda i: (0, 0))
    return pl.pallas_call(
        pack_kernel,
        grid=(classes // tile,),
        in_specs=[
            pl.BlockSpec(memory_space=pltpu.SMEM),
            pl.BlockSpec((per, 1, LANES), lambda i: (i, 0, 0)),
            pl.BlockSpec((tile, LANES), lambda i: (i, 0)),
            pl.BlockSpec((tile, width), lambda i: (i, 0)),
        ],
        out_specs=(whole(width), whole(width), whole(LANES)),
        out_shape=(
            jax.ShapeDtypeStruct((room, width), bf16),
            jax.ShapeDtypeStruct((room, width), bf16),
            jax.ShapeDtypeStruct((room, LANES), f32),
        ),
        compiler_params=params(20),
        cost_estimate=pl.CostEstimate(flops=5 * classes * LANES * width, bytes_accessed=4 * classes * width, transcendentals=0),
        name="pack",
    )(off, row, cnt, centres)


def tiles_used(off, tile):
    return lax.shift_right_logical(off[0, off.shape[1] - 1] + tile - 1, tile.bit_length() - 1)


def last_used(i, off, tile):
    return lax.max(lax.min(i, tiles_used(off, tile) - 1), 0)


def logits_kernel(chunks, tile, off_ref, e0_ref, e1_ref, what_ref, num_ref, at_ref, *refs):
    l0_refs, l1_refs = refs[:chunks], refs[chunks : 2 * chunks]
    w_hbm, den_ref, turn_ref, x_ref, d_acc, w_buf, w_sem = refs[2 * chunks :]
    group, rows_here, _ = l0_refs[0].shape
    rows = 2 * (group + 1) * rows_here
    for j in range(chunks):
        for r, (early, late) in enumerate(((e0_ref, l0_refs[j]), (e1_ref, l1_refs[j]))):
            to = j * rows + r * rows_here
            x_ref[to : to + rows_here, :] = early[j, :rows_here, :]
            for z in range(group):
                to = j * rows + (2 * z + 2 + r) * rows_here
                x_ref[to : to + rows_here, :] = late[z]
    d_acc[...] = jnp.zeros_like(d_acc)
    steps = tiles_used(off_ref, tile)
    half = tile // 2
    cut = rows

    def put(t):
        slot = lax.bitwise_and(t, 1)
        here = pl.ds(pl.multiple_of(t * tile, tile), tile)
        return pltpu.make_async_copy(w_buf.at[slot], w_hbm.at[here], w_sem.at[slot])

    def weigh(first, size, j, slot):
        here = pl.ds(pl.multiple_of(first, half), size)
        ids = iota((size, LANES), 0) + first
        num = num_ref[here, :]
        num_t = num + (math.exp(-logit_scale * margin) - 1.0)
        at = at_ref[j]
        for left in range(0, rows, cut):
            x = x_ref[pl.ds(pl.multiple_of(j * rows + left, cut), cut), :]
            cos = dot(what_ref[here, :], x, 1, 1)
            for k in range(0, cut, LANES):
                cols = slice(left + k, left + k + LANES)
                w = jnp.exp2(cos[:, k : k + LANES]) * jnp.where(ids == at[:, cols], num_t, num)
                d_acc[j, :, cols] += jnp.sum(w.reshape(size // 8, 8, LANES), axis=0)
                w_buf[slot, :size, pl.ds(pl.multiple_of(j * rows + left + k, LANES), LANES)] = w.astype(bf16)

    def one(t, size):
        @pl.when(t >= 2)
        def _():
            put(t - 2).wait()

        slot = lax.bitwise_and(t, 1)
        if size < tile:
            w_buf[slot, size:, :] = jnp.zeros((tile - size, w_buf.shape[2]), bf16)

        together = math.gcd(chunks, 4)

        def chunk(j, carry):
            for k in range(together):
                weigh(t * tile, size, j * together + k, slot)
            return carry

        lax.fori_loop(0, chunks // together, chunk, 0)
        put(t).start()

    def full(t, carry):
        one(t, tile)
        return carry

    used = off_ref[0, off_ref.shape[1] - 1]
    whole = lax.shift_right_logical(used + half - 1, tile.bit_length() - 1)
    lax.fori_loop(0, whole, full, 0)

    @pl.when(whole < steps)
    def _():
        one(whole, half)

    for back in (2, 1):

        @pl.when(steps >= back)
        def _():
            put(steps - back).wait()

    for j in range(chunks):
        den = jnp.sum(d_acc[j], axis=0, keepdims=True)
        den_ref[j] = den
        turn_ref[j] = swap_groups(den, rows_here)


def logits(off, early0, early1, late0, late1, what, num, at, tile, classes):
    chunks = len(late0)
    group, rows_here, width = late0[0].shape
    rows = 2 * (group + 1) * rows_here
    vm = pl.BlockSpec(memory_space=pltpu.VMEM)
    return pl.pallas_call(
        lambda *refs: logits_kernel(chunks, tile, *refs),
        in_specs=[pl.BlockSpec(memory_space=pltpu.SMEM)] + [vm] * (5 + 2 * chunks),
        out_specs=(HBM, vm, vm, vm),
        out_shape=(
            pltpu.HBM((classes, chunks * rows), bf16),
            jax.ShapeDtypeStruct((chunks, 1, rows), f32),
            jax.ShapeDtypeStruct((chunks, 1, rows), f32),
            jax.ShapeDtypeStruct((chunks * rows, width), bf16),
        ),
        scratch_shapes=[
            pltpu.VMEM((chunks, 8, rows), f32),
            pltpu.VMEM((2, tile, chunks * rows), bf16),
            pltpu.SemaphoreType.DMA((2,)),
        ],
        compiler_params=params(8 + 3 * chunks // 2),
        cost_estimate=pl.CostEstimate(
            flops=chunks * rows * classes * width,
            bytes_accessed=chunks * rows * classes + classes * width,
            transcendentals=chunks * rows * classes // 2,
        ),
        name="logits",
    )(off, early0, early1, what, num, at, *late0, *late1)


def own_columns(tile, own, at):
    return pl.BlockSpec((tile, own), lambda i, off: (last_used(i, off, tile), at))


def rows_kernel(chunks, off_ref, what_ref, at_ref, *refs):
    w_refs, (self_ref, away_ref), acc = refs[:chunks], refs[chunks : chunks + 2], refs[chunks + 2]
    i = pl.program_id(0)
    tile = what_ref.shape[0]
    own = w_refs[0].shape[1]
    half = own // 2

    @pl.when(i == 0)
    def _():
        acc[...] = jnp.zeros_like(acc)

    left = off_ref[0, off_ref.shape[1] - 1] - i * tile

    def add(size):
        ids = iota((size, own), 0) + i * tile
        a = [w[:size, :] for w in w_refs] + [ones_where(ids == at_ref[j][:, :own]) for j in range(chunks)]
        acc[...] += dot(jnp.concatenate(a, axis=1), what_ref[:size, :], 0, 0)

    quarter = tile // 4
    for size in range(quarter, tile + 1, quarter):
        fits = left > size - quarter if size == tile else (left > size - quarter) & (left <= size)

        @pl.when(fits)
        def _():
            add(size)

    @pl.when(i == pl.num_programs(0) - 1)
    def _():
        for j in range(chunks):
            for part in range(2):
                at = (part * chunks + j) * own
                self_ref[j, part * half : (part + 1) * half, :] = acc[at : at + half, :].astype(bf16)
                away_ref[j, part * half : (part + 1) * half, :] = acc[at + half : at + own, :].astype(bf16)


def row_parts(off, what, at, w, own, tile):
    chunks, _, rows = at.shape
    width = what.shape[1]
    out = jax.ShapeDtypeStruct((chunks, own, width), bf16)
    whole = pl.BlockSpec((chunks, own, width), lambda i, n: (0, 0, 0))
    return pl.pallas_call(
        lambda *refs: rows_kernel(chunks, *refs),
        grid_spec=pltpu.PrefetchScalarGridSpec(
            num_scalar_prefetch=1,
            grid=(w.shape[0] // tile,),
            in_specs=[
                pl.BlockSpec((tile, width), lambda i, off: (last_used(i, off, tile), 0)),
                pl.BlockSpec(at.shape, lambda i, n: (0, 0, 0)),
            ]
            + [own_columns(tile, own, j * rows // own) for j in range(chunks)],
            out_specs=(whole, whole),
            scratch_shapes=[pltpu.VMEM((2 * chunks * own, width), f32)],
        ),
        out_shape=(out, out),
        compiler_params=params(8 + 3 * chunks),
        cost_estimate=pl.CostEstimate(
            flops=2 * chunks * own * w.shape[0] * width, bytes_accessed=2 * what.size, transcendentals=0
        ),
        name="rows",
    )(off, what, at, *[w] * chunks)


def update_kernel(chunks, step, tile, off_ref, at_ref, rep_ref, raw_ref, c_hbm, m_hbm, *refs):
    w_hbm, x_ref, d_refs = refs[0], refs[1], refs[2 : 2 + chunks]
    mo_hbm, co_hbm, scale_ref, rate_ref, dw_ref, c_buf, m_buf, c_new, m_new, buf, w_sem, c_sem, m_sem, co_sem, mo_sem = refs[2 + chunks :]
    classes, width = c_buf.shape
    per = tile // LANES
    groups = classes // tile
    blocks = off_ref.shape[1] // 2
    rows = x_ref.shape[0] // chunks
    used = off_ref[0, 2 * blocks - 1]

    def span(g):
        return pl.ds(pl.multiple_of(g * tile, tile), tile)

    def ins(g):
        at = span(g)
        return (
            pltpu.make_async_copy(c_hbm.at[at], c_buf.at[at], c_sem.at[g]),
            pltpu.make_async_copy(m_hbm.at[at], m_buf.at[at], m_sem.at[g]),
        )

    def outs(g):
        at, slot = span(g), lax.bitwise_and(g, OUT - 1)
        return (
            pltpu.make_async_copy(c_new.at[slot], co_hbm.at[at], co_sem.at[slot]),
            pltpu.make_async_copy(m_new.at[slot], mo_hbm.at[at], mo_sem.at[slot]),
        )

    def fetch(start):
        slot = lax.bitwise_and(lax.shift_right_logical(start, step.bit_length() - 1), 1)
        at = pl.ds(pl.multiple_of(start, step), step)
        return slot, pltpu.make_async_copy(w_hbm.at[at], buf.at[slot], w_sem.at[slot])

    for first in (0, step):

        @pl.when(used > first)
        def _():
            fetch(first)[1].start()

    for g in range(groups):
        for copy in ins(g):
            copy.start()
    for j in range(chunks):
        den = d_refs[0][j]
        for q in range(1, chunks):
            den = den + d_refs[q][j ^ q]
        rate = logit_scale / den
        rate_ref[j] = rate.astype(bf16)
        if j == 0:
            scale_ref[...] = rate

    def work(done, size):
        slot = lax.bitwise_and(lax.shift_right_logical(done, step.bit_length() - 1), 1)
        at = pl.ds(pl.multiple_of(done, step), size)
        exact = min(size, 256)
        ids = iota((exact, rows), 0).astype(f32).astype(bf16)
        lines = []
        for h in range(0, size, exact):
            parts = []
            for j in range(chunks):
                place = at_ref[j] - (done + h)
                place = jnp.where((place >= 0) & (place < exact), place, -1).astype(f32).astype(bf16)
                g = buf[slot, h : h + exact, j * rows : (j + 1) * rows] * rate_ref[j]
                parts.append(jnp.where(ids == place, g - jnp.asarray(logit_scale, bf16), g))
            lines.append(jnp.concatenate(parts, axis=1))
        dw = dot(jnp.concatenate(lines, axis=0), x_ref[...], 1, 0)
        c = raw_ref[at, :].astype(f32)
        inv = 1.0 / jnp.sqrt(jnp.sum(c * c, axis=1, keepdims=True) + eps)
        along = jnp.sum(c * dw, axis=1, keepdims=True) * (inv * inv)
        dw_ref[at, :] = ((dw - c * along) * (inv * (1.0 / sharpness))).astype(bf16)
        dw_ref[pl.ds(pl.multiple_of(done + size, size), 2 * LANES), :] = jnp.zeros((2 * LANES, width), bf16)

    def one(done):
        fetch(done)[1].wait()

        @pl.when(used - done > step // 2)
        def _():
            work(done, step)

        @pl.when(used - done <= step // 2)
        def _():
            work(done, step // 2)

        @pl.when(done + 2 * step < used)
        def _():
            fetch(done + 2 * step)[1].start()

        return done + step

    def group(g, done):
        done = lax.while_loop(lambda d: d < off_ref[0, blocks + (g + 1) * per - 1], one, done)
        for copy in ins(g):
            copy.wait()
        slot = lax.bitwise_and(g, OUT - 1)

        @pl.when(g >= OUT)
        def _():
            for copy in outs(g - OUT):
                copy.wait()

        lane = iota((LANES, LANES), 1)
        for k in range(per):
            base = pl.multiple_of(lax.shift_left(lax.shift_right_logical(off_ref[0, g * per + k], 4), 4), 16)
            mine = pl.ds(pl.multiple_of(g * tile + k * LANES, LANES), LANES)
            to = slice(k * LANES, (k + 1) * LANES)
            place = rep_ref[mine, :] - base
            place = jnp.concatenate([ones_where(place == lane), ones_where(place == lane + LANES)], axis=1)
            dw = dot(place, dw_ref[pl.ds(base, 2 * LANES), :], 1, 0)
            c = c_buf[mine, :].astype(f32)
            m = momentum_rate * m_buf[mine, :] + dw + weight_decay * c
            m_new[slot, to, :] = m
            c_new[slot, to, :] = (c - learn_rate * m).astype(bf16)
        for copy in outs(g):
            copy.start()
        return done

    @pl.when(used == 0)
    def _():
        dw_ref[: 2 * LANES, :] = jnp.zeros((2 * LANES, width), bf16)

    lax.fori_loop(0, groups, group, 0)
    for g in range(max(0, groups - OUT), groups):
        for copy in outs(g):
            copy.wait()


def update(off, at, rep, raw, centres, momentum, w, x, dens, tile, step):
    chunks = len(dens)
    classes, width = centres.shape
    rows = x.shape[0] // chunks
    vm = pl.BlockSpec(memory_space=pltpu.VMEM)
    sems = pltpu.SemaphoreType.DMA((classes // tile,))
    return pl.pallas_call(
        lambda *refs: update_kernel(chunks, step, tile, *refs),
        in_specs=[pl.BlockSpec(memory_space=pltpu.SMEM), vm, vm, vm, HBM, HBM, HBM] + [vm] * (1 + chunks),
        out_specs=(HBM, HBM, vm),
        out_shape=(
            jax.ShapeDtypeStruct((classes, width), f32),
            jax.ShapeDtypeStruct((classes, width), bf16),
            jax.ShapeDtypeStruct((1, rows), f32),
        ),
        scratch_shapes=[
            pltpu.VMEM((chunks, 1, rows), bf16),
            pltpu.VMEM((classes + 2 * LANES + step, width), bf16),
            pltpu.VMEM((classes, width), bf16),
            pltpu.VMEM((classes, width), f32),
            pltpu.VMEM((OUT, tile, width), bf16),
            pltpu.VMEM((OUT, tile, width), f32),
            pltpu.VMEM((2, step, chunks * rows), bf16),
            pltpu.SemaphoreType.DMA((2,)),
            sems,
            sems,
            pltpu.SemaphoreType.DMA((OUT,)),
            pltpu.SemaphoreType.DMA((OUT,)),
        ],
        compiler_params=params(22 + 3 * chunks),
        cost_estimate=pl.CostEstimate(
            flops=rows * chunks * classes * width,
            bytes_accessed=rows * chunks * classes + 12 * classes * width,
            transcendentals=0,
        ),
        name="update",
    )(off, at, rep, raw, centres, momentum, w, x, *dens)


def body(embeddings, labels, centres, momentum, sample_home, sample_row):
    shards = lax.axis_size("cls")
    group = lax.axis_size("dp")
    chips = shards // 2
    home_rows, _ = centres.shape
    rows_here = embeddings.shape[0]
    here = sample_row.shape[0]
    classes, sampled = shards * home_rows, shards * here
    shard = lax.axis_index("cls")

    dims = (home_rows, rows_here, here, classes, sampled)
    told = tell(embeddings, sample_home, sample_row, labels, dims)

    from_z = []
    for m in [1, group - 1] + list(range(2, group - 1)):
        from_z.append(shift(told, "dp", m))
    early = jnp.stack([told] + [swap(told, "cls", 2 * q) for q in range(1, chips)])
    early_away = swap(early, "cls", 1)
    late0 = jnp.stack([z[:rows_here] for z in from_z])
    late = [late0]
    for q in range(1, chips):
        late.append(swap(late0, "cls", 2 * q))
    late_away = []
    for x in late:
        late_away.append(swap(x, "cls", 1))

    me = shard.astype(jnp.int32).reshape(1)
    in_hbm = lambda x: pltpu.with_memory_space_constraint(x, pltpu.HBM)
    row, rep, cnt, off, known, table = prepare(me, early, early_away, dims)
    what, raw, num = pack(off, row, cnt, in_hbm(centres), min(1024, home_rows))
    at = label_places(me, known, table, [told] + from_z, chips, dims)
    tile = min(512, home_rows)
    w, own_den, turned, x = logits(off, early, early_away, late, late_away, what, num, at, tile, home_rows)
    w = in_hbm(w)

    den = own_den + swap(turned, "cls", 1)
    dens = [den] + [swap(den, "cls", 2 * q) for q in range(1, chips)]

    self_part, away_part = row_parts(off, what, at, w, 2 * rows_here, min(1024, home_rows))
    pair = self_part.astype(f32) + swap(away_part, "cls", 1).astype(f32)
    sums = [swap(pair[q].astype(bf16), "cls", 2 * q) for q in range(1, chips)]

    momentum_new, centres_new, scale = update(
        off, at, rep, raw, in_hbm(centres), in_hbm(momentum), w, x, dens, min(512, home_rows), 512
    )
    total = pair[0]
    for got in sums:
        total = total + got.astype(f32)
    xfloat = embeddings.astype(f32)
    row_norm = jnp.sqrt(jnp.sum(xfloat * xfloat, axis=1, keepdims=True) + eps)
    unit = xfloat / row_norm
    scale = scale[0, :rows_here][:, None]
    dunit = total[:rows_here] * scale - logit_scale * total[rows_here:]
    emb_grad = (dunit - unit * jnp.sum(unit * dunit, axis=1, keepdims=True)) / row_norm
    return (emb_grad, momentum_new, centres_new)


def solution(mesh):
    placed = (
        P(("dp", "cls"), None),
        P("dp"),
        P("cls", None),
        P("cls", None),
        P("cls", None),
        P("cls"),
    )
    return jax.shard_map(
        body,
        mesh=mesh,
        in_specs=placed,
        out_specs=(P(("dp", "cls"), None), P("cls", None), P("cls", None)),
        check_vma=False,
    )
```

```python
import math

import jax
import jax.numpy as jnp
from jax import lax
from jax.experimental import pallas as pl
from jax.experimental.pallas import tpu as pltpu
from jax.sharding import PartitionSpec as P

eps = 1e-06
logit_scale = 64.0
margin = 0.35
momentum_rate = 0.9
learn_rate = 0.1
weight_decay = 0.0005

LANES = 128
OUT = 4
sharpness = logit_scale * math.log2(math.e)
HBM = pl.BlockSpec(memory_space=pltpu.HBM)
bf16 = jnp.bfloat16
f32 = jnp.float32


def dot(a, b, ca, cb):
    return lax.dot_general(a, b, (((ca,), (cb,)), ((), ())), preferred_element_type=f32)


def swap(x, axis_name, m):
    n = lax.axis_size(axis_name)
    return lax.ppermute(x, axis_name, [(i, i ^ m) for i in range(n)])


def shift(x, axis_name, m):
    n = lax.axis_size(axis_name)
    return lax.ppermute(x, axis_name, [(i, (i + m) % n) for i in range(n)])


def params(mib):
    return pltpu.CompilerParams(vmem_limit_bytes=mib << 20)


def iota(shape, axis):
    return lax.broadcasted_iota(jnp.int32, shape, axis)


def ones_where(mask):
    return mask.astype(f32).astype(bf16)


def look_up(table, hi, lo, limit):
    n_hi, n = table.shape[0], hi.shape[1]
    oh = ones_where(iota((n_hi, n), 0) == hi)
    got = jnp.zeros((LANES, n), f32)
    for bits in range(0, 8 * pieces_of(limit), 8):
        piece = lax.bitwise_and(lax.shift_right_logical(table, bits), 255).astype(f32).astype(bf16)
        got = got + float(1 << bits) * dot(piece, oh, 0, 0)
    pick = jnp.where(iota((LANES, n), 0) == lo, got, 0.0)
    return jnp.sum(pick, axis=0, keepdims=True).astype(jnp.int32)


def pieces_of(limit):
    return -(-(limit - 1).bit_length() // 8)


def tell_kernel(dims, x_ref, home_ref, row_ref, lab_ref, o_ref):
    home_rows, rows_here, _, classes, sampled = dims
    width = x_ref.shape[1]
    x = x_ref[...].astype(f32)
    scale = sharpness / jnp.sqrt(jnp.sum(x * x, axis=1, keepdims=True) + eps)
    o_ref[:rows_here, :] = (x * scale).astype(bf16)
    per = width // LANES
    lines = []
    for values, limit in ((home_ref[...] * home_rows + row_ref[...], classes), (lab_ref[...], sampled)):
        for k in range(pieces_of(limit)):
            v = lax.bitwise_and(lax.shift_right_logical(values, 8 * k), 255).astype(f32)
            for r in range(v.shape[0] // per):
                lines.append(jnp.concatenate([v[r * per + c : r * per + c + 1, :] for c in range(per)], axis=1))
    lines += [jnp.zeros_like(lines[0])] * (o_ref.shape[0] - rows_here - len(lines))
    o_ref[rows_here:, :] = jnp.concatenate(lines, axis=0).astype(bf16)


def tell(embeddings, home, row, labels, dims):
    _, rows_here, _, classes, sampled = dims
    width = embeddings.shape[1]
    lines = (row.size * pieces_of(classes) + labels.size * pieces_of(sampled)) // width
    args = [embeddings, home.reshape(-1, LANES), row.reshape(-1, LANES), labels.reshape(-1, LANES)]
    args = [pltpu.with_memory_space_constraint(x, pltpu.HBM) for x in args]
    return pl.pallas_call(
        lambda *refs: tell_kernel(dims, *refs),
        out_shape=jax.ShapeDtypeStruct((-(-(rows_here + lines) // 16) * 16, width), bf16),
        compiler_params=params(4),
        name="tell",
    )(*args)


def decode(get, row, count, number):
    total = get(row, row + count).astype(f32)
    for k in range(1, number):
        total = total + float(1 << (8 * k)) * get(row + k * count, row + (k + 1) * count).astype(f32)
    return total


def swap_groups(x, size):
    n = x.shape[1] // size
    return jnp.concatenate([x[:, (g ^ 1) * size : ((g ^ 1) + 1) * size] for g in range(n)], axis=1)


def prep_kernel(dims, shard_ref, mine_ref, away_ref, row_ref, rep_ref, cnt_ref, off_ref, known_ref, table_ref):
    home_rows, rows_here, here, classes, _ = dims
    base = shard_ref[0] * home_rows
    chips, _, width = mine_ref.shape
    blocks = home_rows // LANES
    lines, id_bytes = here // width, pieces_of(classes)
    total = jnp.zeros((LANES, blocks), f32)
    total_t = jnp.zeros((blocks, LANES), f32)
    for tile in range(2 * chips):
        ref = (mine_ref, away_ref)[tile % 2]
        ids = decode(lambda p, q: ref[tile // 2, p:q, :], rows_here, lines, id_bytes).astype(jnp.int32)
        h = ids - base
        for k in range(lines):
            a = ones_where(iota((blocks, width), 0) == lax.shift_right_arithmetic(h[k : k + 1], 7))
            b = ones_where(iota((LANES, width), 0) == lax.bitwise_and(h[k : k + 1], LANES - 1))
            total = total + dot(b, a, 1, 1)
            total_t = total_t + dot(a, b, 1, 1)
            for c in range(width // LANES):
                to = (tile * lines + k) * (width // LANES) + c
                table_ref[to : to + 1, :] = ids[k : k + 1, c * LANES : (c + 1) * LANES]
    have, have_t = ones_where(total > 0), ones_where(total_t > 0)
    before = ones_where(iota((LANES, LANES), 1) < iota((LANES, LANES), 0))
    ahead = ones_where(iota((LANES, LANES), 0) < iota((LANES, LANES), 1))
    ahead_b = ones_where(iota((blocks, blocks), 0) < iota((blocks, blocks), 1))
    before_b = ones_where(iota((blocks, blocks), 1) < iota((blocks, blocks), 0))
    sizes = jnp.broadcast_to(jnp.sum(have.astype(f32), axis=0, keepdims=True), (8, blocks))
    start = dot(sizes.astype(bf16), ahead_b, 1, 0)
    off_ref[...] = jnp.concatenate([start, start + sizes], axis=1).astype(jnp.int32)
    sizes_t = jnp.broadcast_to(jnp.sum(have_t.astype(f32), axis=1, keepdims=True), (blocks, LANES))
    start_t = dot(before_b, sizes_t.astype(bf16), 1, 0)
    pos = jnp.where(total > 0, dot(before, have, 1, 0) + start[:1], -1.0).astype(jnp.int32)
    pos_t = jnp.where(total_t > 0, dot(have_t, ahead, 1, 0) + start_t, -1.0).astype(jnp.int32)
    for k in range(blocks):
        rows = slice(k * LANES, (k + 1) * LANES)
        row_ref[k] = pos_t[k : k + 1, :]
        rep_ref[rows, :] = jnp.broadcast_to(pos[:, k : k + 1], (LANES, LANES))
        cnt_ref[rows, :] = jnp.broadcast_to(total[:, k : k + 1], (LANES, LANES))
    known_ref[...] = jnp.maximum(pos_t, 0)


def labels_kernel(dims, shard_ref, known_ref, table_ref, *refs):
    home_rows, rows_here, here, classes, sampled = dims
    z_refs, at_ref = refs[:-1], refs[-1]
    chips = at_ref.shape[0]
    width = z_refs[0].shape[1]
    shard = shard_ref[0]
    base = shard * home_rows
    lines, id_bytes = here // width, pieces_of(classes)
    known = known_ref[...]
    table = table_ref[...]
    own = 2 * rows_here
    group_rows = 2 * chips * rows_here
    lab_lines, lab_bytes = group_rows // width, pieces_of(sampled)
    per_tile = here // LANES
    for z, ref in enumerate(z_refs):
        first = rows_here + lines * id_bytes
        got = decode(lambda p, q: ref[p:q, :], first, lab_lines, lab_bytes)
        lab = jnp.concatenate([got[k : k + 1] for k in range(lab_lines)], axis=1)
        bit = 1
        while bit < 2 * chips:
            lab = jnp.where(lax.bitwise_and(shard, bit) != 0, swap_groups(lab, bit * rows_here), lab)
            bit *= 2
        lab = lab.astype(jnp.int32)
        tile = lax.bitwise_xor(lax.shift_right_logical(lab, here.bit_length() - 1), shard)
        hi = tile * per_tile + lax.shift_right_logical(lax.bitwise_and(lab, here - 1), 7)
        h = look_up(table, hi, lax.bitwise_and(lab, LANES - 1), classes) - base
        at = look_up(known, lax.shift_right_arithmetic(h, 7), lax.bitwise_and(h, LANES - 1), home_rows)
        at = jnp.where((h >= 0) & (h < home_rows), at, -1)
        for j in range(chips):
            at_ref[j, :, z * own : (z + 1) * own] = at[:, j * own : (j + 1) * own]


def prepare(shard, mine, away, dims):
    home_rows, _, _, _, sampled = dims
    vm = pl.BlockSpec(memory_space=pltpu.VMEM)
    blocks = home_rows // LANES
    i32 = jnp.int32
    return pl.pallas_call(
        lambda *refs: prep_kernel(dims, *refs),
        in_specs=[pl.BlockSpec(memory_space=pltpu.SMEM), vm, vm],
        out_specs=(vm,) * 6,
        out_shape=(
            jax.ShapeDtypeStruct((blocks, 1, LANES), i32),
            jax.ShapeDtypeStruct((home_rows, LANES), i32),
            jax.ShapeDtypeStruct((home_rows, LANES), f32),
            jax.ShapeDtypeStruct((8, 2 * blocks), i32),
            jax.ShapeDtypeStruct((blocks, LANES), i32),
            jax.ShapeDtypeStruct((sampled // LANES, LANES), i32),
        ),
        compiler_params=params(10),
        cost_estimate=pl.CostEstimate(flops=128 * sampled * LANES, bytes_accessed=1024 * home_rows, transcendentals=0),
        name="prep",
    )(shard, mine, away)


def label_places(shard, known, table, told, chips, dims):
    rows_here = dims[1]
    vm = pl.BlockSpec(memory_space=pltpu.VMEM)
    return pl.pallas_call(
        lambda *refs: labels_kernel(dims, *refs),
        in_specs=[pl.BlockSpec(memory_space=pltpu.SMEM)] + [vm] * (2 + len(told)),
        out_specs=vm,
        out_shape=jax.ShapeDtypeStruct((chips, 1, 2 * len(told) * rows_here), jnp.int32),
        compiler_params=params(12),
        cost_estimate=pl.CostEstimate(
            flops=8 * table.size * 2 * chips * len(told) * rows_here, bytes_accessed=8 * table.size, transcendentals=0
        ),
        name="places",
    )(shard, known, table, *told)


WINDOW = LANES + 16


def pack_kernel(off_ref, row_ref, cnt_ref, c_ref, what_ref, raw_ref, num_ref):
    i = pl.program_id(0)

    @pl.when(i == 0)
    def _():
        for ref in (what_ref, raw_ref, num_ref):
            ref[:16, :] = jnp.zeros((16, ref.shape[1]), ref.dtype)

    c = c_ref[...].astype(f32)
    width = c.shape[1]
    unit = (c * (1.0 / jnp.sqrt(jnp.sum(c * c, axis=1, keepdims=True) + eps))).astype(bf16)
    cnt = cnt_ref[...]
    high = jnp.floor(cnt * (1.0 / 256.0))
    low = cnt - 256.0 * high
    here = row_ref.shape[0]
    todo = []
    for k in range(here):
        rows = slice(k * LANES, (k + 1) * LANES)
        base = pl.multiple_of(lax.shift_left(lax.shift_right_logical(off_ref[0, i * here + k], 4), 4), 16)
        pick = ones_where(iota((WINDOW, LANES), 0) + base == row_ref[k])
        right = jnp.concatenate([unit[rows], c_ref[rows, :], low[rows].astype(bf16), high[rows].astype(bf16)], axis=1)
        todo.append((base, dot(pick, right, 1, 0)))
    for base, got in todo:
        num = got[:, 2 * width : 2 * width + LANES] + 256.0 * got[:, 2 * width + LANES :]
        for ref, new in ((what_ref, got[:, :width]), (raw_ref, got[:, width : 2 * width]), (num_ref, num)):
            new = new.astype(ref.dtype)
            ref[pl.ds(base, 16), :] = ref[pl.ds(base, 16), :] + new[:16]
            ref[pl.ds(pl.multiple_of(base + 16, 16), LANES), :] = new[16:]

    @pl.when(i == pl.num_programs(0) - 1)
    def _():
        for ref in (what_ref, raw_ref, num_ref):
            ref[pl.ds(pl.multiple_of(base + WINDOW, 16), 4 * LANES), :] = jnp.zeros((4 * LANES, ref.shape[1]), ref.dtype)


def pack(off, row, cnt, centres, tile):
    classes, width = centres.shape
    per = tile // LANES
    room = classes + 6 * LANES
    whole = lambda n: pl.BlockSpec((room, n), lambda i: (0, 0))
    return pl.pallas_call(
        pack_kernel,
        grid=(classes // tile,),
        in_specs=[
            pl.BlockSpec(memory_space=pltpu.SMEM),
            pl.BlockSpec((per, 1, LANES), lambda i: (i, 0, 0)),
            pl.BlockSpec((tile, LANES), lambda i: (i, 0)),
            pl.BlockSpec((tile, width), lambda i: (i, 0)),
        ],
        out_specs=(whole(width), whole(width), whole(LANES)),
        out_shape=(
            jax.ShapeDtypeStruct((room, width), bf16),
            jax.ShapeDtypeStruct((room, width), bf16),
            jax.ShapeDtypeStruct((room, LANES), f32),
        ),
        compiler_params=params(20),
        cost_estimate=pl.CostEstimate(flops=5 * classes * LANES * width, bytes_accessed=4 * classes * width, transcendentals=0),
        name="pack",
    )(off, row, cnt, centres)


def tiles_used(off, tile):
    return lax.shift_right_logical(off[0, off.shape[1] - 1] + tile - 1, tile.bit_length() - 1)


def last_used(i, off, tile):
    return lax.max(lax.min(i, tiles_used(off, tile) - 1), 0)


def logits_kernel(chunks, tile, off_ref, e0_ref, e1_ref, what_ref, num_ref, at_ref, *refs):
    l0_refs, l1_refs = refs[:chunks], refs[chunks : 2 * chunks]
    w_hbm, den_ref, turn_ref, x_ref, d_acc, w_buf, w_sem = refs[2 * chunks :]
    group, rows_here, _ = l0_refs[0].shape
    rows = 2 * (group + 1) * rows_here
    for j in range(chunks):
        for r, (early, late) in enumerate(((e0_ref, l0_refs[j]), (e1_ref, l1_refs[j]))):
            to = j * rows + r * rows_here
            x_ref[to : to + rows_here, :] = early[j, :rows_here, :]
            for z in range(group):
                to = j * rows + (2 * z + 2 + r) * rows_here
                x_ref[to : to + rows_here, :] = late[z]
    d_acc[...] = jnp.zeros_like(d_acc)
    steps = tiles_used(off_ref, tile)
    half = tile // 2
    cut = rows

    def put(t):
        slot = lax.bitwise_and(t, 1)
        here = pl.ds(pl.multiple_of(t * tile, tile), tile)
        return pltpu.make_async_copy(w_buf.at[slot], w_hbm.at[here], w_sem.at[slot])

    def weigh(first, size, j, slot):
        here = pl.ds(pl.multiple_of(first, half), size)
        ids = iota((size, LANES), 0) + first
        num = num_ref[here, :]
        num_t = num + (math.exp(-logit_scale * margin) - 1.0)
        at = at_ref[j]
        for left in range(0, rows, cut):
            x = x_ref[pl.ds(pl.multiple_of(j * rows + left, cut), cut), :]
            cos = dot(what_ref[here, :], x, 1, 1)
            for k in range(0, cut, LANES):
                cols = slice(left + k, left + k + LANES)
                w = jnp.exp2(cos[:, k : k + LANES]) * jnp.where(ids == at[:, cols], num_t, num)
                d_acc[j, :, cols] += jnp.sum(w.reshape(size // 8, 8, LANES), axis=0)
                w_buf[slot, :size, pl.ds(pl.multiple_of(j * rows + left + k, LANES), LANES)] = w.astype(bf16)

    def one(t, size):
        @pl.when(t >= 2)
        def _():
            put(t - 2).wait()

        slot = lax.bitwise_and(t, 1)
        if size < tile:
            w_buf[slot, size:, :] = jnp.zeros((tile - size, w_buf.shape[2]), bf16)

        together = math.gcd(chunks, 4)

        def chunk(j, carry):
            for k in range(together):
                weigh(t * tile, size, j * together + k, slot)
            return carry

        lax.fori_loop(0, chunks // together, chunk, 0)
        put(t).start()

    def full(t, carry):
        one(t, tile)
        return carry

    used = off_ref[0, off_ref.shape[1] - 1]
    whole = lax.shift_right_logical(used + half - 1, tile.bit_length() - 1)
    lax.fori_loop(0, whole, full, 0)

    @pl.when(whole < steps)
    def _():
        one(whole, half)

    for back in (2, 1):

        @pl.when(steps >= back)
        def _():
            put(steps - back).wait()

    for j in range(chunks):
        den = jnp.sum(d_acc[j], axis=0, keepdims=True)
        den_ref[j] = den
        turn_ref[j] = swap_groups(den, rows_here)


def logits(off, early0, early1, late0, late1, what, num, at, tile, classes):
    chunks = len(late0)
    group, rows_here, width = late0[0].shape
    rows = 2 * (group + 1) * rows_here
    vm = pl.BlockSpec(memory_space=pltpu.VMEM)
    return pl.pallas_call(
        lambda *refs: logits_kernel(chunks, tile, *refs),
        in_specs=[pl.BlockSpec(memory_space=pltpu.SMEM)] + [vm] * (5 + 2 * chunks),
        out_specs=(HBM, vm, vm, vm),
        out_shape=(
            pltpu.HBM((classes, chunks * rows), bf16),
            jax.ShapeDtypeStruct((chunks, 1, rows), f32),
            jax.ShapeDtypeStruct((chunks, 1, rows), f32),
            jax.ShapeDtypeStruct((chunks * rows, width), bf16),
        ),
        scratch_shapes=[
            pltpu.VMEM((chunks, 8, rows), f32),
            pltpu.VMEM((2, tile, chunks * rows), bf16),
            pltpu.SemaphoreType.DMA((2,)),
        ],
        compiler_params=params(8 + 3 * chunks // 2),
        cost_estimate=pl.CostEstimate(
            flops=chunks * rows * classes * width,
            bytes_accessed=chunks * rows * classes + classes * width,
            transcendentals=chunks * rows * classes // 2,
        ),
        name="logits",
    )(off, early0, early1, what, num, at, *late0, *late1)


def own_columns(tile, own, at):
    return pl.BlockSpec((tile, own), lambda i, off: (last_used(i, off, tile), at))


def rows_kernel(chunks, off_ref, what_ref, at_ref, *refs):
    w_refs, (self_ref, away_ref), acc = refs[:chunks], refs[chunks : chunks + 2], refs[chunks + 2]
    i = pl.program_id(0)
    tile = what_ref.shape[0]
    own = w_refs[0].shape[1]
    half = own // 2

    @pl.when(i == 0)
    def _():
        acc[...] = jnp.zeros_like(acc)

    left = off_ref[0, off_ref.shape[1] - 1] - i * tile

    def add(size):
        ids = iota((size, own), 0) + i * tile
        a = [w[:size, :] for w in w_refs] + [ones_where(ids == at_ref[j][:, :own]) for j in range(chunks)]
        acc[...] += dot(jnp.concatenate(a, axis=1), what_ref[:size, :], 0, 0)

    quarter = tile // 4
    for size in range(quarter, tile + 1, quarter):
        fits = left > size - quarter if size == tile else (left > size - quarter) & (left <= size)

        @pl.when(fits)
        def _():
            add(size)

    @pl.when(i == pl.num_programs(0) - 1)
    def _():
        for j in range(chunks):
            for part in range(2):
                at = (part * chunks + j) * own
                self_ref[j, part * half : (part + 1) * half, :] = acc[at : at + half, :].astype(bf16)
                away_ref[j, part * half : (part + 1) * half, :] = acc[at + half : at + own, :].astype(bf16)


def row_parts(off, what, at, w, own, tile):
    chunks, _, rows = at.shape
    width = what.shape[1]
    out = jax.ShapeDtypeStruct((chunks, own, width), bf16)
    whole = pl.BlockSpec((chunks, own, width), lambda i, n: (0, 0, 0))
    return pl.pallas_call(
        lambda *refs: rows_kernel(chunks, *refs),
        grid_spec=pltpu.PrefetchScalarGridSpec(
            num_scalar_prefetch=1,
            grid=(w.shape[0] // tile,),
            in_specs=[
                pl.BlockSpec((tile, width), lambda i, off: (last_used(i, off, tile), 0)),
                pl.BlockSpec(at.shape, lambda i, n: (0, 0, 0)),
            ]
            + [own_columns(tile, own, j * rows // own) for j in range(chunks)],
            out_specs=(whole, whole),
            scratch_shapes=[pltpu.VMEM((2 * chunks * own, width), f32)],
        ),
        out_shape=(out, out),
        compiler_params=params(8 + 3 * chunks),
        cost_estimate=pl.CostEstimate(
            flops=2 * chunks * own * w.shape[0] * width, bytes_accessed=2 * what.size, transcendentals=0
        ),
        name="rows",
    )(off, what, at, *[w] * chunks)


def update_kernel(chunks, step, tile, off_ref, at_ref, rep_ref, raw_ref, c_hbm, m_hbm, *refs):
    w_hbm, x_ref, d_refs = refs[0], refs[1], refs[2 : 2 + chunks]
    mo_hbm, co_hbm, scale_ref, rate_ref, dw_ref, c_buf, m_buf, c_new, m_new, buf, w_sem, c_sem, m_sem, co_sem, mo_sem = refs[2 + chunks :]
    classes, width = c_buf.shape
    per = tile // LANES
    groups = classes // tile
    blocks = off_ref.shape[1] // 2
    rows = x_ref.shape[0] // chunks
    used = off_ref[0, 2 * blocks - 1]

    def span(g):
        return pl.ds(pl.multiple_of(g * tile, tile), tile)

    def ins(g):
        at = span(g)
        return (
            pltpu.make_async_copy(c_hbm.at[at], c_buf.at[at], c_sem.at[g]),
            pltpu.make_async_copy(m_hbm.at[at], m_buf.at[at], m_sem.at[g]),
        )

    def outs(g):
        at, slot = span(g), lax.bitwise_and(g, OUT - 1)
        return (
            pltpu.make_async_copy(c_new.at[slot], co_hbm.at[at], co_sem.at[slot]),
            pltpu.make_async_copy(m_new.at[slot], mo_hbm.at[at], mo_sem.at[slot]),
        )

    def fetch(start):
        slot = lax.bitwise_and(lax.shift_right_logical(start, step.bit_length() - 1), 1)
        at = pl.ds(pl.multiple_of(start, step), step)
        return slot, pltpu.make_async_copy(w_hbm.at[at], buf.at[slot], w_sem.at[slot])

    for first in (0, step):

        @pl.when(used > first)
        def _():
            fetch(first)[1].start()

    for g in range(groups):
        for copy in ins(g):
            copy.start()
    for j in range(chunks):
        den = d_refs[0][j]
        for q in range(1, chunks):
            den = den + d_refs[q][j ^ q]
        rate = logit_scale / den
        rate_ref[j] = rate.astype(bf16)
        if j == 0:
            scale_ref[...] = rate

    def work(done, size):
        slot = lax.bitwise_and(lax.shift_right_logical(done, step.bit_length() - 1), 1)
        at = pl.ds(pl.multiple_of(done, step), size)
        exact = min(size, 256)
        ids = iota((exact, rows), 0).astype(f32).astype(bf16)
        lines = []
        for h in range(0, size, exact):
            parts = []
            for j in range(chunks):
                place = at_ref[j] - (done + h)
                place = jnp.where((place >= 0) & (place < exact), place, -1).astype(f32).astype(bf16)
                g = buf[slot, h : h + exact, j * rows : (j + 1) * rows] * rate_ref[j]
                parts.append(jnp.where(ids == place, g - jnp.asarray(logit_scale, bf16), g))
            lines.append(jnp.concatenate(parts, axis=1))
        dw = dot(jnp.concatenate(lines, axis=0), x_ref[...], 1, 0)
        c = raw_ref[at, :].astype(f32)
        inv = 1.0 / jnp.sqrt(jnp.sum(c * c, axis=1, keepdims=True) + eps)
        along = jnp.sum(c * dw, axis=1, keepdims=True) * (inv * inv)
        dw_ref[at, :] = ((dw - c * along) * (inv * (1.0 / sharpness))).astype(bf16)
        dw_ref[pl.ds(pl.multiple_of(done + size, size), 2 * LANES), :] = jnp.zeros((2 * LANES, width), bf16)

    def apply(g):
        slot = lax.bitwise_and(g, OUT - 1)
        lane = iota((LANES, LANES), 1)
        for k in range(per):
            base = pl.multiple_of(lax.shift_left(lax.shift_right_logical(off_ref[0, g * per + k], 4), 4), 16)
            mine = pl.ds(pl.multiple_of(g * tile + k * LANES, LANES), LANES)
            to = slice(k * LANES, (k + 1) * LANES)
            place = rep_ref[mine, :] - base
            place = jnp.concatenate([ones_where(place == lane), ones_where(place == lane + LANES)], axis=1)
            dw = dot(place, dw_ref[pl.ds(base, 2 * LANES), :], 1, 0)
            c = c_buf[mine, :].astype(f32)
            m = momentum_rate * m_buf[mine, :] + dw + weight_decay * c
            m_new[slot, to, :] = m
            c_new[slot, to, :] = (c - learn_rate * m).astype(bf16)

    def ready(g):
        for copy in ins(g):
            copy.wait()

        @pl.when(g >= OUT)
        def _():
            for copy in outs(g - OUT):
                copy.wait()

    def send(g):
        for copy in outs(g):
            copy.start()

    def ahead(done):
        @pl.when(done + 2 * step < used)
        def _():
            fetch(done + 2 * step)[1].start()

    @pl.when(used == 0)
    def _():
        dw_ref[: 2 * LANES, :] = jnp.zeros((2 * LANES, width), bf16)

    def turn(state):
        done, g = state
        can = off_ref[0, blocks + (g + 1) * per - 1] <= done
        full = used - done > step // 2
        both = can & full

        @pl.when(both)
        def _():
            ready(g)
            fetch(done)[1].wait()
            apply(g)
            work(done, step)
            send(g)
            ahead(done)

        @pl.when(can & jnp.logical_not(full))
        def _():
            ready(g)
            apply(g)
            send(g)

        @pl.when(jnp.logical_not(can))
        def _():
            fetch(done)[1].wait()

            @pl.when(full)
            def _():
                work(done, step)

            @pl.when(jnp.logical_not(full))
            def _():
                work(done, step // 2)

            ahead(done)

        tile_done = both | jnp.logical_not(can)
        return done + jnp.where(tile_done, step, 0), g + jnp.where(can, 1, 0)

    lax.while_loop(lambda state: state[1] < groups, turn, (jnp.int32(0), jnp.int32(0)))
    for g in range(max(0, groups - OUT), groups):
        for copy in outs(g):
            copy.wait()


def update(off, at, rep, raw, centres, momentum, w, x, dens, tile, step):
    chunks = len(dens)
    classes, width = centres.shape
    rows = x.shape[0] // chunks
    vm = pl.BlockSpec(memory_space=pltpu.VMEM)
    sems = pltpu.SemaphoreType.DMA((classes // tile,))
    return pl.pallas_call(
        lambda *refs: update_kernel(chunks, step, tile, *refs),
        in_specs=[pl.BlockSpec(memory_space=pltpu.SMEM), vm, vm, vm, HBM, HBM, HBM] + [vm] * (1 + chunks),
        out_specs=(HBM, HBM, vm),
        out_shape=(
            jax.ShapeDtypeStruct((classes, width), f32),
            jax.ShapeDtypeStruct((classes, width), bf16),
            jax.ShapeDtypeStruct((1, rows), f32),
        ),
        scratch_shapes=[
            pltpu.VMEM((chunks, 1, rows), bf16),
            pltpu.VMEM((classes + 2 * LANES + step, width), bf16),
            pltpu.VMEM((classes, width), bf16),
            pltpu.VMEM((classes, width), f32),
            pltpu.VMEM((OUT, tile, width), bf16),
            pltpu.VMEM((OUT, tile, width), f32),
            pltpu.VMEM((2, step, chunks * rows), bf16),
            pltpu.SemaphoreType.DMA((2,)),
            sems,
            sems,
            pltpu.SemaphoreType.DMA((OUT,)),
            pltpu.SemaphoreType.DMA((OUT,)),
        ],
        compiler_params=params(22 + 3 * chunks),
        cost_estimate=pl.CostEstimate(
            flops=rows * chunks * classes * width,
            bytes_accessed=rows * chunks * classes + 12 * classes * width,
            transcendentals=0,
        ),
        name="update",
    )(off, at, rep, raw, centres, momentum, w, x, *dens)


def body(embeddings, labels, centres, momentum, sample_home, sample_row):
    shards = lax.axis_size("cls")
    group = lax.axis_size("dp")
    chips = shards // 2
    home_rows, _ = centres.shape
    rows_here = embeddings.shape[0]
    here = sample_row.shape[0]
    classes, sampled = shards * home_rows, shards * here
    shard = lax.axis_index("cls")

    dims = (home_rows, rows_here, here, classes, sampled)
    told = tell(embeddings, sample_home, sample_row, labels, dims)

    from_z = []
    for m in [1, group - 1] + list(range(2, group - 1)):
        from_z.append(shift(told, "dp", m))
    early = jnp.stack([told] + [swap(told, "cls", 2 * q) for q in range(1, chips)])
    early_away = swap(early, "cls", 1)
    late0 = jnp.stack([z[:rows_here] for z in from_z])
    late = [late0]
    for q in range(1, chips):
        late.append(swap(late0, "cls", 2 * q))
    late_away = []
    for x in late:
        late_away.append(swap(x, "cls", 1))

    me = shard.astype(jnp.int32).reshape(1)
    in_hbm = lambda x: pltpu.with_memory_space_constraint(x, pltpu.HBM)
    row, rep, cnt, off, known, table = prepare(me, early, early_away, dims)
    what, raw, num = pack(off, row, cnt, in_hbm(centres), min(2048, home_rows))
    at = label_places(me, known, table, [told] + from_z, chips, dims)
    tile = min(512, home_rows)
    w, own_den, turned, x = logits(off, early, early_away, late, late_away, what, num, at, tile, home_rows)
    w = in_hbm(w)

    den = own_den + swap(turned, "cls", 1)
    dens = [den] + [swap(den, "cls", 2 * q) for q in range(1, chips)]

    self_part, away_part = row_parts(off, what, at, w, 2 * rows_here, min(1024, home_rows))
    pair = self_part.astype(f32) + swap(away_part, "cls", 1).astype(f32)
    sums = [swap(pair[q].astype(bf16), "cls", 2 * q) for q in range(1, chips)]

    momentum_new, centres_new, scale = update(
        off, at, rep, raw, in_hbm(centres), in_hbm(momentum), w, x, dens, min(512, home_rows), 512
    )
    total = pair[0]
    for got in sums:
        total = total + got.astype(f32)
    xfloat = embeddings.astype(f32)
    row_norm = jnp.sqrt(jnp.sum(xfloat * xfloat, axis=1, keepdims=True) + eps)
    unit = xfloat / row_norm
    scale = scale[0, :rows_here][:, None]
    dunit = total[:rows_here] * scale - logit_scale * total[rows_here:]
    emb_grad = (dunit - unit * jnp.sum(unit * dunit, axis=1, keepdims=True)) / row_norm
    return (emb_grad, momentum_new, centres_new)


def solution(mesh):
    placed = (
        P(("dp", "cls"), None),
        P("dp"),
        P("cls", None),
        P("cls", None),
        P("cls", None),
        P("cls"),
    )
    return jax.shard_map(
        body,
        mesh=mesh,
        in_specs=placed,
        out_specs=(P(("dp", "cls"), None), P("cls", None), P("cls", None)),
        check_vma=False,
    )
```
